32 devices in a mesh: grp: 2 (over core), gx: 4 (over z), gy: 4 (over y, x).
Axes of the slice: x: 2, y: 2, z: 4, core: 2. Of those that a mesh axis runs over, the one named last changes fastest.
Arguments:
- fields: float32 [2, 3, 128, 512], P('grp', None, 'gx', 'gy'), may hold values from -6 to 6
- coefficients: float32 [2, 128, 512], P('grp', 'gx', 'gy'), may hold values from 0.05 to 0.24
- forcing: float32 [2, 3, 128, 512], P('grp', None, 'gx', 'gy'), may hold values from -4 to 4
- element_matrix: float32 [12, 12], replicated, as said below
- source_cells: int32 [2, 1024, 128], P('grp', ('gx', 'gy')), may hold values from 0 to 4095
- target_cells: int32 [2, 1024, 128], P('grp', ('gx', 'gy')), may hold values from 0 to 4095
- peer_map: int32 [2, 1024, 1], P('grp', ('gx', 'gy')), may hold values from 0 to 15; in each aligned block of 64 rows (0 to 63, 64 to 127, ..., all dimensions but the last counted through in order) at most 8 rows name the same one
- mapping_blocks: bfloat16 [2, 1024, 128, 128], P('grp', ('gx', 'gy')), may hold values from -0.25 to 0.25
Outputs:
- new_fields: float32 [2, 3, 128, 512], P('grp', None, 'gx', 'gy')
- interface_load: float32 [2, 3, 128, 512], P('grp', None, 'gx', 'gy')
The draws below stay inside these ranges and needn't reach their ends.
Inputs may be any that keep to these rules, and one draw needn't show every extreme that they name: `peer_map`: within the 64 blocks of one partition no receiving partition is named more than 8 times. `source_cells`: local point indices of the sending partition. `target_cells`: local point indices of the receiving partition. `element_matrix`: Symmetric; every diagonal entry exceeds the sum of magnitudes of the other entries of its row by 0.5 or more.
All inputs are finite; a program needn't handle non-finite values.
Results may differ from the reference program's by a relative error of at most 0.012.
Values sent between devices are 32-bit elements; how exact they have to be, the bound alone decides.
A program may use at most 128 MiB of HBM per device.

```python
import math
import jax
import jax.numpy as jnp
import numpy as np
from jax import lax

CX = 32
CY = 128
NBLK = 64
BLOCK = 128
ITERS = 4
SUB = 4
PARTS_SIZE = 16
CAP = 8
NX = 128
NY = 512
N_GX = 4
N_GY = 4


def draw_element_matrix(key, part):
    first, second = jax.random.split(jax.random.fold_in(key, 11))
    rough = jax.random.normal(first, (12, 12), jnp.float32) * 0.25
    symmetric = 0.5 * (rough + rough.T)
    offdiag = symmetric * (1.0 - jnp.eye(12, dtype=jnp.float32))
    margin = jax.random.uniform(second, (12,), jnp.float32, 0.5, 1.5)
    return offdiag + jnp.diag(jnp.sum(jnp.abs(offdiag), axis=1) + margin)


def touch_ends(result, key, low, top_value):
    longest = result.shape.index(max(result.shape))
    spots = []
    for shift in (0, 1):
        where = [jax.random.randint(jax.random.fold_in(key, axis), (), 0, length) for axis, length in enumerate(result.shape)]
        where[longest] = (where[longest] + shift) % result.shape[longest]
        spots.append(tuple(where))
    return result.at[spots[0]].set(low).at[spots[1]].set(top_value)


def steps_of(stream_key, dims, cuts, smallest, largest):
    factor_of, own = 1.0, jax.random.fold_in(stream_key, 6)
    for axis_at, parts in cuts:
        heights = jnp.exp(jax.random.uniform(jax.random.fold_in(own, axis_at), (parts,), jnp.float32, smallest / len(cuts), largest / len(cuts)))
        factor_of = factor_of * jnp.repeat(heights, dims[axis_at] // parts).reshape([-1 if axis == axis_at else 1 for axis in range(len(dims))])
    return factor_of


def deal_out(own_key, own, number, rows, count, top, most, skew):
    ranking = jax.random.permutation(own_key, count)
    crowded, ordinary = shares(count, rows * top, most, skew, True), shares(count, rows * top, most, skew, False)
    places = jnp.arange(count)

    def named(sizes, turn):
        used = int((sizes > 0).sum())
        fixed = max(1, used // 4)
        passed = fixed + (places - fixed + turn * (used - fixed)) % max(1, count - fixed)
        return jnp.zeros((count,), jnp.int32).at[ranking[jnp.where(places < fixed, places, passed)]].set(jnp.asarray(sizes, jnp.int32))

    sizes = jnp.where(number % 4 == 0, named(crowded, number // 4), named(ordinary, number - number // 4 - 1))
    mixed = jax.random.permutation(jax.random.fold_in(own, 3), count)
    source_of, receiver = mixed[0:count // 2 * 2:2], mixed[1:count // 2 * 2:2]
    room = jnp.minimum(sizes[source_of] - 1, most - sizes[receiver]) // 2
    room = jnp.where((source_of == ranking[0]) | (receiver == ranking[0]) | (sizes[receiver] == 0), 0, jnp.maximum(room, 0))
    passed = jax.random.randint(jax.random.fold_in(own, 4), (count // 2,), 0, 1 << 20) % (room + 1)
    sizes = sizes.at[source_of].add(-passed).at[receiver].add(passed)
    items = jnp.searchsorted(jnp.cumsum(sizes), jnp.arange(rows * top), side="right").astype(jnp.int32)
    grid = items.reshape(top, rows).T
    grid = grid[jax.random.permutation(jax.random.fold_in(own, 1), rows)]
    turn = jax.random.randint(jax.random.fold_in(own, 2), (rows, 1), 0, top)
    return jnp.take_along_axis(grid, (jnp.arange(top)[None, :] + turn) % top, axis=1)


def shares(amount, total, reach, skew, full):
    loads = [(1 << 20) // math.isqrt(rank ** skew) + 1 for rank in range(1, amount + 1)]
    largest = reach if full else min(reach, max(-(-total // amount), total * loads[0] // sum(loads)))
    least = 1 if total - largest >= amount - 1 else 0
    counts, spare = [largest] + [least] * (amount - 1), total - largest - least * (amount - 1)
    while spare > 0:
        free = [i for i in range(1, amount) if counts[i] < largest] or [i for i in range(1, amount) if counts[i] < reach]
        mass, left = sum([loads[i] for i in free]), spare
        for i in free:
            addition = min(reach - counts[i], max(1, left * loads[i] // mass), spare)
            counts[i] = counts[i] + addition
            spare = spare - addition
    return np.array(counts)


def noise(stream_key, extent, deviation, limit, cuts=(), kind=jnp.bfloat16):
    factor_of = steps_of(stream_key, extent, cuts, -0.22, 0.18) if cuts else 1.0
    values = jax.random.normal(stream_key, extent, jnp.float32) * deviation * factor_of
    return jnp.minimum(jnp.maximum(values, -limit), limit).astype(kind)


def setup_inputs(seed: int = 0) -> dict:
    key_of = jax.random.split(jax.random.key(seed), 9)
    fields = noise(key_of[0], (2, 3, NX, NY), 1.0, 6.0, ((0, 2), (2, 4), (3, 4)), jnp.float32)
    coefficients = jnp.clip(jnp.exp(math.log(0.24) - 1.5686159 * jax.random.uniform(key_of[1], (2, NX, NY), jnp.float32) ** steps_of(key_of[1], (2, NX, NY), ((0, 2), (1, 4), (2, 4)), -0.2, 0.2)), 0.05, 0.24)
    forcing = noise(key_of[2], (2, 3, NX, NY), 0.3, 4.0, ((0, 2), (2, 4), (3, 4)), jnp.float32)
    element_matrix = draw_element_matrix(jax.random.fold_in(key_of[8], 71), 0)
    source_cells = touch_ends(jax.random.randint(key_of[4], (2, PARTS_SIZE * NBLK, BLOCK), 0, CX * CY), jax.random.fold_in(key_of[4], 1), 0, (CX * CY) - 1).astype(jnp.int32)
    target_cells = touch_ends(jax.random.randint(key_of[5], (2, PARTS_SIZE * NBLK, BLOCK), 0, CX * CY), jax.random.fold_in(key_of[5], 1), 0, (CX * CY) - 1).astype(jnp.int32)
    peer_map_keys = jax.random.split(jax.random.fold_in(key_of[6], 1), 2 * (PARTS_SIZE * NBLK) // NBLK)
    peer_map_turns = jax.random.permutation(jax.random.fold_in(key_of[6], 3), 2 * (PARTS_SIZE * NBLK) // NBLK)
    peer_map = jax.vmap(lambda own, number: deal_out(jax.random.fold_in(key_of[6], 2), own, number, NBLK, N_GX * N_GY, 1, CAP, 2))(peer_map_keys, peer_map_turns).reshape((2, PARTS_SIZE * NBLK, 1))
    mapping_blocks = noise(key_of[7], (2, PARTS_SIZE * NBLK, BLOCK, BLOCK), (4 * BLOCK) ** -0.5, 0.25, ((0, 2), (1, 16)))
    return dict(fields=fields, coefficients=coefficients, forcing=forcing, element_matrix=element_matrix, source_cells=source_cells, target_cells=target_cells, peer_map=peer_map, mapping_blocks=mapping_blocks)


DT_STEP = 1.0
RELAX = 0.6


def fluid_sweep(padded, viscous, forcing, applied):
    centre = padded[:, 1:-1, 1:-1]
    middle = viscous[1:-1, 1:-1]
    flux_sum = 0.5 * (middle + viscous[2:, 1:-1]) * (padded[:, 2:, 1:-1] - centre)
    flux_sum = flux_sum + 0.5 * (middle + viscous[:-2, 1:-1]) * (padded[:, :-2, 1:-1] - centre)
    flux_sum = flux_sum + 0.5 * (middle + viscous[1:-1, 2:]) * (padded[:, 1:-1, 2:] - centre)
    flux_sum = flux_sum + 0.5 * (middle + viscous[1:-1, :-2]) * (padded[:, 1:-1, :-2] - centre)
    return centre + DT_STEP * (flux_sum + forcing + applied)


def shell_sweep(padded, stiff_pad, element_matrix, forcing, applied):
    stiffness = stiff_pad[:-1, :-1]
    nodal = jnp.concatenate([padded[:, :-1, :-1], padded[:, 1:, :-1], padded[:, :-1, 1:], padded[:, 1:, 1:]], axis=0)
    element_force = jnp.einsum("ab,bxy->axy", element_matrix, nodal, precision=lax.Precision.HIGHEST) * stiffness
    nodal_force = element_force[0:3, 1:, 1:] + element_force[3:6, :-1, 1:]
    nodal_force = nodal_force + element_force[6:9, 1:, :-1] + element_force[9:12, :-1, :-1]
    diag_terms = jnp.diagonal(element_matrix)
    diagonal = diag_terms[0:3, None, None] * stiffness[None, 1:, 1:] + diag_terms[3:6, None, None] * stiffness[None, :-1, 1:]
    diagonal = diagonal + diag_terms[6:9, None, None] * stiffness[None, 1:, :-1] + diag_terms[9:12, None, None] * stiffness[None, :-1, :-1]
    return padded[:, 1:-1, 1:-1] + RELAX * (forcing + applied - nodal_force) / diagonal


def blocks_of(values):
    comps = values.shape[0]
    shaped = values.reshape(comps, N_GX, CX, N_GY, CY).transpose(1, 3, 0, 2, 4)
    return shaped.reshape(N_GX * N_GY, comps, CX * CY)


def grid_of(blocks):
    comps = blocks.shape[1]
    shaped = blocks.reshape(N_GX, N_GY, comps, CX, CY).transpose(2, 0, 3, 1, 4)
    return shaped.reshape(comps, CX * N_GX, CY * N_GY)


def outgoing(values, source_cells, mapping_blocks):
    partitions = N_GX * N_GY
    parted = blocks_of(values)

    def per_part(pieces):
        local, cells, matrices = pieces
        read = local[:, cells].astype(jnp.bfloat16).astype(jnp.float32)
        return jnp.einsum("cln,lnm->lcm", read, matrices.astype(jnp.float32))

    mapped = lax.map(per_part, (parted, source_cells.reshape(partitions, NBLK, BLOCK), mapping_blocks.reshape(partitions, NBLK, BLOCK, BLOCK)))
    return mapped.reshape(partitions * NBLK, 3, BLOCK)


def incoming(mapped, peer_map, target_cells):
    partitions = N_GX * N_GY
    where = (peer_map[:, 0:1] * (CX * CY) + target_cells).astype(jnp.int32)
    flat = jnp.zeros((3, partitions * CX * CY), jnp.float32)
    flat = flat.at[:, where.reshape(-1)].add(mapped.transpose(1, 0, 2).reshape(3, -1))
    return grid_of(flat.reshape(3, partitions, CX * CY).transpose(1, 0, 2))


def reference(fields, coefficients, forcing, element_matrix, source_cells, target_cells, peer_map, mapping_blocks):
    fluid_field = fields[0]
    shell_field = fields[1]
    viscous = jnp.pad(coefficients[0], 1)
    stiff_pad = jnp.pad(coefficients[1], 1)
    applied = jnp.zeros((2, 3, CX * N_GX, CY * N_GY), jnp.float32)
    edges = ((0, 0), (1, 1), (1, 1))
    for outer in range(ITERS):
        for inner in range(SUB):
            fluid_field = fluid_sweep(jnp.pad(fluid_field, edges), viscous, forcing[0], applied[0])
            shell_field = shell_sweep(jnp.pad(shell_field, edges), stiff_pad, element_matrix, forcing[1], applied[1])
        to_shell = incoming(outgoing(fluid_field, source_cells[0], mapping_blocks[0]), peer_map[0], target_cells[0])
        to_fluid = incoming(outgoing(shell_field, source_cells[1], mapping_blocks[1]), peer_map[1], target_cells[1])
        applied = jnp.stack([to_fluid, to_shell])
    return jnp.stack([fluid_field, shell_field]), applied
```

```python
import functools

import jax
import jax.numpy as jnp
from jax import lax
from jax.experimental import pallas as pl
from jax.experimental.pallas import tpu as pltpu
from jax.sharding import PartitionSpec as P

ITERS = 4
SUB = 4
DT_STEP = 1.0
RELAX = 0.6
ROWS = 8
LANES = 128
F32 = jnp.float32
BF16 = jnp.bfloat16


def iota(shape, dim):
    return lax.broadcasted_iota(jnp.int32, shape, dim)


def shift(value, amount, axis):
    return pltpu.roll(value, amount % value.shape[axis], axis)


def one_hot(mask):
    return jnp.where(mask, 1.0, 0.0).astype(BF16)


def fold_rows(blocks):
    row = iota(blocks[0].shape, 0)
    stride = 1
    while len(blocks) > 1:
        low = row % (2 * stride) < stride
        blocks = [
            jnp.where(low, a, b) + shift(jnp.where(low, b, a), stride, 0)
            for a, b in zip(blocks[::2], blocks[1::2])
        ]
        stride *= 2
    return blocks[0]


def kernel(
    parts_x,
    parts_y,
    field_ref,
    coef_ref,
    force_ref,
    element_ref,
    source_ref,
    target_ref,
    peer_ref,
    map_hbm,
    field_out,
    load_out,
    state,
    wave,
    load,
    base,
    stat,
    row_send,
    col_send,
    row_recv,
    col_recv,
    corner_recv,
    load_row_send,
    load_col_send,
    load_row_recv,
    load_col_recv,
    load_corner_recv,
    spread,
    value_send,
    value_recv,
    index_send,
    index_recv,
    info,
    info_scalar,
    map_ref,
    pick_cols,
    pick_rows,
    place_cols,
    place_rows,
    halo_ss,
    halo_rs,
    load_ss,
    load_rs,
    value_ss,
    value_rs,
    index_ss,
    index_rs,
    map_sem,
    info_sem,
):
    comps, cells_x, cells_y = field_ref.shape[1:]
    links, width = source_ref.shape[1:]
    parts = parts_x * parts_y
    slots = parts * ROWS
    chunks = links // ROWS
    half_x = cells_x // 2
    span = ROWS * width
    ext_x, ext_y = state.shape[1:]
    group = lax.axis_index("grp")
    gx = lax.axis_index("gx")
    gy = lax.axis_index("gy")
    me = gx * parts_y + gy
    mesh_id = pl.DeviceIdType.MESH

    def peer_device(q):
        return {"grp": 1 - group, "gx": lax.div(q, parts_y), "gy": lax.rem(q, parts_y)}

    halves = 2 if parts_x % 2 == 0 else 1
    half = parts_x // halves

    def partner_of(k, sign):
        turn = halves - 1 - lax.div(k, half * parts_y)
        within = lax.rem(k, half * parts_y)
        along = lax.rem(lax.rem(gx, half) + sign * lax.div(within, parts_y) + half, half)
        x = lax.rem(lax.div(gx, half) + turn, halves) * half + along
        y = lax.rem(gy + sign * lax.rem(within, parts_y) + parts_y, parts_y)
        return x * parts_y + y

    def turn_of(q):
        x, y = lax.div(q, parts_y), lax.rem(q, parts_y)
        turn = halves - 1 - lax.rem(lax.div(x, half) - lax.div(gx, half) + halves, halves)
        along = lax.rem(lax.rem(x, half) - lax.rem(gx, half) + half, half)
        return (turn * half + along) * parts_y + lax.rem(y - gy + parts_y, parts_y)

    def inside(dx, dy):
        ok = None
        for pos, step, size in ((gx, dx, parts_x), (gy, dy, parts_y)):
            if step:
                test = (pos + step >= 0) & (pos + step < size)
                ok = test if ok is None else ok & test
        return ok

    steps = ((1, 0), (-1, 0), (0, -1), (0, 1), (-1, -1), (-1, 1), (1, -1), (1, 1))

    for ref in (row_recv, col_recv, corner_recv, load_row_recv, load_col_recv, load_corner_recv):
        ref[...] = jnp.zeros_like(ref)

    barrier = pltpu.get_barrier_semaphore()

    def greet(k, carry):
        q = lax.rem(me + k, parts)
        pl.semaphore_signal(barrier, inc=1, device_id=peer_device(q), device_id_type=mesh_id)
        return carry

    lax.fori_loop(0, parts, greet, 0)
    for dx, dy in steps:

        @pl.when(inside(dx, dy))
        def _(dx=dx, dy=dy):
            pl.semaphore_signal(
                barrier, inc=1, device_id={"gx": gx + dx, "gy": gy + dy}, device_id_type=mesh_id
            )

    pltpu.make_async_copy(map_hbm, map_ref, map_sem).start()

    def as_col(row):
        square = iota((links, links), 0) == iota((links, links), 1)
        return jnp.sum(jnp.where(square, row, 0.0), axis=1, keepdims=True)

    key_row = turn_of(peer_ref[0]).astype(F32)
    key_col = as_col(key_row)
    below, lane = iota((links, links), 0), iota((links, links), 1)
    same = (key_col == key_row) & (below < lane)
    rank_row = jnp.sum(jnp.where(same, 1.0, 0.0), axis=0, keepdims=True)
    ahead = jnp.where(same | (key_col < key_row), 1.0, 0.0)
    pos_row = jnp.sum(ahead, axis=0, keepdims=True)
    pos_col = as_col(pos_row)
    order = jnp.sum(
        jnp.where(pos_col.astype(jnp.int32) == iota((links, LANES), 1), iota((links, LANES), 0), 0),
        axis=0,
        keepdims=True,
    )
    info[0:1, :LANES] = order
    first = jnp.where(key_col.astype(jnp.int32) < iota((links, info.shape[1]), 1), 1, 0)
    info[1:2, :] = jnp.sum(first, axis=0, keepdims=True)
    info_copy = pltpu.make_async_copy(info, info_scalar, info_sem)
    info_copy.start()

    slot_row = (key_row * ROWS + rank_row).astype(jnp.int32)
    to_slot = one_hot(iota((slots, links), 0) == slot_row)
    target = target_ref[0]
    target_x = (target // cells_y + 1).astype(F32).astype(BF16)
    target_y = (target % cells_y).astype(F32).astype(BF16)
    index = cells_y * (jnp.dot(to_slot, target_x, preferred_element_type=F32) - 1.0)
    index = index + jnp.dot(to_slot, target_y, preferred_element_type=F32)
    index_send[...] = index.reshape(parts, ROWS, width)

    to_place = one_hot(iota((links, links), 0) == pos_row.astype(jnp.int32))
    source = source_ref[0]
    source_y = (source // (half_x * cells_y)) * cells_y + source % cells_y
    source_x = (source // cells_y) % half_x
    sorted_y = jnp.dot(to_place, source_y.astype(F32).astype(BF16), preferred_element_type=F32)
    sorted_x = jnp.dot(to_place, source_x.astype(F32).astype(BF16), preferred_element_type=F32)
    sorted_y = sorted_y.astype(jnp.int32)
    pick_rows[...] = sorted_x.astype(jnp.int32)
    for i in range(links):
        hot = iota((2 * cells_y, width), 0) == sorted_y[i : i + 1]
        pick_cols[i // ROWS, :, i % ROWS * width : (i % ROWS + 1) * width] = one_hot(hot)
    spread[...] = jnp.zeros_like(spread)
    wave[...] = jnp.zeros_like(wave)

    def index_copy(k, q):
        return pltpu.make_async_remote_copy(
            src_ref=index_send.at[k],
            dst_ref=index_recv.at[k],
            send_sem=index_ss.at[k],
            recv_sem=index_rs.at[k],
            device_id=peer_device(q),
            device_id_type=mesh_id,
        )

    def value_copy(k, q, par):
        return pltpu.make_async_remote_copy(
            src_ref=value_send.at[k],
            dst_ref=value_recv.at[par, k],
            send_sem=value_ss.at[k],
            recv_sem=value_rs.at[par, k],
            device_id=peer_device(q),
            device_id_type=mesh_id,
        )

    field_halo = (row_send, col_send, row_recv, col_recv, corner_recv, halo_ss, halo_rs)
    load_halo = (load_row_send, load_col_send, load_row_recv, load_col_recv, load_corner_recv, load_ss, load_rs)

    def halo_copy(halo, d, par, count):
        rows, cols, rows_in, cols_in, corners_in, send, recv = halo
        dx, dy = steps[d]
        if d < 2:
            source, place = rows.at[1 - d, pl.ds(0, count)], rows_in.at[par, d, pl.ds(0, count)]
        elif d < 4:
            source, place = cols, cols_in.at[par, d - 2]
        else:
            edge = pl.ds(0, ROWS) if d < 6 else pl.ds(cells_x - ROWS, ROWS)
            source, place = cols.at[edge], corners_in.at[par, d - 4]
        return pltpu.make_async_remote_copy(
            src_ref=source,
            dst_ref=place,
            send_sem=send.at[d],
            recv_sem=recv.at[par, d],
            device_id={"gx": gx + dx, "gy": gy + dy},
            device_id_type=mesh_id,
        )

    def halo_start(halo, par, centres):
        rows, cols = halo[:2]
        lane = iota((cells_x, cells_y), 1)
        packed = jnp.zeros((cells_x, cells_y), F32)
        for q, centre in enumerate(centres):
            rows[0, q] = centre[:ROWS]
            rows[1, q] = centre[cells_x - ROWS :]
            low = (lane >= 8 * q) & (lane < 8 * q + 4)
            high = (lane >= 8 * q + 4) & (lane < 8 * q + 8)
            packed = jnp.where(low, shift(centre, 8 * q, 1), packed)
            packed = jnp.where(high, shift(centre, 8 * q + 8, 1), packed)
        cols[...] = packed
        for d, (dx, dy) in reversed(list(enumerate(steps))):

            @pl.when(inside(dx, dy))
            def _(d=d):
                halo_copy(halo, d, par, len(centres)).start()

    def halo_finish(halo, par, centres):
        rows_in, cols_in, corners_in = halo[2:5]
        for d, (dx, dy) in enumerate(steps):

            @pl.when(inside(-dx, -dy))
            def _(d=d):
                halo_copy(halo, d, par, len(centres)).wait_recv()

        upper = iota((ROWS, cells_y), 0) < SUB
        ends = [
            jnp.where(upper, corners_in[par, 0], corners_in[par, 2]),
            jnp.where(upper, corners_in[par, 1], corners_in[par, 3]),
        ]
        east = jnp.concatenate([cols_in[par, 0], ends[0]], axis=0)
        west = jnp.concatenate([cols_in[par, 1], ends[1]], axis=0)
        lane = iota((ext_x, cells_y), 1)
        wide = []
        for q, centre in enumerate(centres):
            end = jnp.where(upper, rows_in[par, 1, q], rows_in[par, 0, q])
            side = jnp.where(lane >= cells_y - SUB, shift(west, -8 * q - 8, 1), 0.0)
            side = jnp.where(lane < SUB, shift(east, -8 * q, 1), side)
            middle = jnp.concatenate([centre, end], axis=0)
            wide.append(jnp.where(keep, jnp.concatenate([middle, side], axis=1), 0.0))
        return wide

    def halo_sent(halo, count):
        for d, (dx, dy) in enumerate(steps):

            @pl.when(inside(dx, dy))
            def _(d=d):
                halo_copy(halo, d, 0, count).wait_send()

    beside_x = jnp.where(gx > 0, 1, 0) + jnp.where(gx < parts_x - 1, 1, 0)
    beside_y = jnp.where(gy > 0, 1, 0) + jnp.where(gy < parts_y - 1, 1, 0)
    pl.semaphore_wait(barrier, parts + (beside_x + 1) * (beside_y + 1) - 1)

    ext_row = iota((ext_x, ext_y), 0)
    ext_col = iota((ext_x, ext_y), 1)
    row_at = jnp.where(ext_row < cells_x + SUB, ext_row, ext_row - ext_x) + gx * cells_x
    near = (ext_col < cells_y + SUB) | (ext_col >= ext_y - SUB)
    col_at = jnp.where(ext_col < cells_y + SUB, ext_col, ext_col - ext_y) + gy * cells_y
    keep = near & (row_at >= 0) & (row_at < cells_x * parts_x)
    keep = keep & (col_at >= 0) & (col_at < cells_y * parts_y)

    start_values = [field_ref[0, c] for c in range(comps)]
    start_values += [force_ref[0, c] for c in range(comps)]
    start_values.append(coef_ref[0])
    halo_start(field_halo, 1, start_values)

    def send_index(k, carry):
        index_copy(k, partner_of(k, 1)).start()
        return carry

    lax.fori_loop(0, parts, send_index, 0)
    info_copy.wait()
    wide = halo_finish(field_halo, 1, start_values)
    for c in range(comps):
        state[c] = wide[c]
        base[c] = wide[comps + c]
    coef = wide[2 * comps]
    halo_sent(field_halo, 2 * comps + 1)

    @pl.when(group == 0)
    def _():
        for k, (amount, axis) in enumerate(((-1, 0), (1, 0), (-1, 1), (1, 1))):
            stat[k] = 0.5 * (coef + shift(coef, amount, axis))

    @pl.when(group == 1)
    def _():
        stat[0] = coef
        north = shift(coef, 1, 0)
        west_coef = shift(coef, 1, 1)
        corner = shift(north, 1, 1)
        for c in range(comps):
            total = 0.0
            for node, near_coef in enumerate((coef, north, west_coef, corner)):
                k = node * comps + c
                total = total + element_ref[k, k] * near_coef
            stat[1 + c] = RELAX / jnp.where(keep, total, 1.0)

    def flow_sweeps(field, rhs, count):
        def sweep(i, carry):
            for c in range(comps):
                v = field[c]
                flux = rhs[c]
                for k, (amount, axis) in enumerate(((-1, 0), (1, 0), (-1, 1), (1, 1))):
                    flux = flux + stat[k] * (shift(v, amount, axis) - v)
                field[c] = jnp.where(keep, v + DT_STEP * flux, 0.0)
            return carry

        lax.fori_loop(0, count, sweep, 0, unroll=True)

    def shell_sweeps(field, rhs, count):
        def sweep(i, carry):
            own = [field[c] for c in range(comps)]
            south = [shift(u, -1, 0) for u in own]
            nodal = own + south
            nodal = nodal + [shift(u, -1, 1) for u in own] + [shift(u, -1, 1) for u in south]
            stiffness = stat[0]

            def force(a):
                total = element_ref[a, 0] * nodal[0]
                for b in range(1, 4 * comps):
                    total = total + element_ref[a, b] * nodal[b]
                return total * stiffness

            for c in range(comps):
                here = force(c) + shift(force(comps + c), 1, 0)
                there = force(2 * comps + c) + shift(force(3 * comps + c), 1, 0)
                total = here + shift(there, 1, 1)
                result = own[c] + (rhs[c] - total) * stat[1 + c]
                field[c] = jnp.where(keep, result, 0.0)
            return carry

        lax.fori_loop(0, count, sweep, 0, unroll=True)

    def sweep_state():
        @pl.when(group == 0)
        def _():
            flow_sweeps(state, base, SUB)

        @pl.when(group == 1)
        def _():
            shell_sweeps(state, base, SUB)

    sweep_state()
    pltpu.make_async_copy(map_hbm, map_ref, map_sem).wait()

    def coupling(t, carry):
        par = lax.rem(t, 2)
        centres = [state[c, :cells_x, :cells_y] + wave[c, :cells_x, :cells_y] for c in range(comps)]
        for c in range(comps):
            field_out[0, c] = centres[c]

        @pl.when(t < ITERS - 1)
        def _():
            halo_start(field_halo, par, [field_out[0, c] for c in range(comps)])

        table = jnp.concatenate(
            [jnp.concatenate([centre[:half_x], centre[half_x:]], axis=1) for centre in centres], axis=0
        ).astype(BF16)

        def pick(i):
            at = i * ROWS
            values = jnp.dot(table, pick_cols[i], preferred_element_type=F32)
            mapped = []
            for k in range(ROWS):
                lanes = slice(k * width, (k + 1) * width)
                in_row = iota((half_x, width), 0) == pick_rows[at + k : at + k + 1]
                read = []
                for c in range(comps):
                    chosen = jnp.where(in_row, values[c * half_x : (c + 1) * half_x, lanes], 0.0)
                    total = chosen[:ROWS]
                    for r in range(ROWS, half_x, ROWS):
                        total = total + chosen[r : r + ROWS]
                    read.append(total)
                read = jnp.concatenate(read, axis=0).astype(BF16)
                block = map_ref[0, info_scalar[0, at + k]]
                mapped.append(jnp.dot(read, block, preferred_element_type=F32))
            for c in range(comps):
                spread[c, at : at + ROWS] = fold_rows([m[c * ROWS : (c + 1) * ROWS] for m in mapped])

        def send(k):
            begin = info_scalar[1, k]
            for c in range(comps):
                value_send[k, c] = spread[c, pl.ds(begin, ROWS), :]
            value_copy(k, partner_of(k, 1), par).start()

        for i in range(chunks):
            pick(i)
            if i < parts:
                send(i)

        def send_rest(k, carry):
            send(k)
            return carry

        lax.fori_loop(min(chunks, parts), parts, send_rest, 0, unroll=4)

        @pl.when(t < ITERS - 1)
        def _():
            centres = [field_out[0, c] for c in range(comps)]
            wide = halo_finish(field_halo, par, centres)
            for c in range(comps):
                state[c] = wide[c]
            sweep_state()
            halo_sent(field_halo, comps)

        @pl.when(t == 0)
        def _():
            def take(k, carry):
                index_copy(k, me).wait_recv()
                where = index_recv[k].astype(jnp.int32)
                in_row = where // cells_y
                where = where % cells_y
                for r in range(ROWS):
                    lanes = slice(r * width, (r + 1) * width)
                    place_rows[k, :, lanes] = one_hot(iota((cells_x, width), 0) == in_row[r : r + 1])
                    mask = jnp.where(iota((cells_y, width), 0) == where[r : r + 1], 1.0, 0.0)
                    place_cols[k, lanes] = mask.T.astype(BF16)
                return carry

            lax.fori_loop(0, parts, take, 0)

        def weigh(k):
            value_copy(k, me, par).wait_recv()
            weighted = []
            for r in range(ROWS):
                in_row = place_rows[k, :, r * width : (r + 1) * width]
                weighted.append(
                    jnp.concatenate(
                        [
                            jnp.broadcast_to(value_recv[par, k, c, r : r + 1], in_row.shape).astype(BF16) * in_row
                            for c in range(comps)
                        ],
                        axis=0,
                    )
                )
            return jnp.concatenate(weighted, axis=1)

        def place(i, total):
            for k in range(1):
                k = lax.rem(i + k + parts // 2, parts)
                total = total + jnp.dot(weigh(k), place_cols[k], preferred_element_type=F32)
            return total

        empty = jnp.zeros((comps * cells_x, cells_y), F32)
        applied = lax.fori_loop(0, parts // 1, place, empty, unroll=4)
        for c in range(comps):
            load_out[0, c] = applied[c * cells_x : (c + 1) * cells_x]

        @pl.when(t < ITERS - 1)
        def _():
            centres = [load_out[0, c] for c in range(comps)]
            halo_start(load_halo, par, centres)
            wide = halo_finish(load_halo, par, centres)
            for c in range(comps):
                load[c] = wide[c]

            @pl.when(group == 0)
            def _():
                for c in range(comps):
                    wave[c] = DT_STEP * load[c]
                flow_sweeps(wave, load, SUB - 1)

            @pl.when(group == 1)
            def _():
                for c in range(comps):
                    wave[c] = load[c] * stat[1 + c]
                shell_sweeps(wave, load, SUB - 1)

            halo_sent(load_halo, comps)

        def sent(k, carry):
            value_copy(k, me, par).wait_send()
            return carry

        lax.fori_loop(0, parts, sent, 0)
        return carry

    lax.fori_loop(0, ITERS, coupling, 0)

    def index_sent(k, carry):
        index_copy(k, me).wait_send()
        return carry

    lax.fori_loop(0, parts, index_sent, 0)


def hand_over(field_ref, load_ref, field_out, load_out):
    field_out[...] = field_ref[...]
    load_out[...] = load_ref[...]


def body(parts_x, parts_y, fields, *rest):
    _, comps, cells_x, cells_y = fields.shape
    links, width = rest[3].shape[1:]
    parts = parts_x * parts_y
    ext = (cells_x + ROWS, cells_y + LANES)
    chunks = links // ROWS
    vmem = pl.BlockSpec(memory_space=pltpu.VMEM)
    dma = pltpu.SemaphoreType.DMA
    rest = (*rest[:5], rest[5].reshape(1, 1, links), rest[6])

    def halo_buffers(arrays):
        return [
            pltpu.VMEM((2, arrays, ROWS, cells_y), F32),
            pltpu.VMEM((cells_x, cells_y), F32),
            pltpu.VMEM((2, 2, arrays, ROWS, cells_y), F32),
            pltpu.VMEM((2, 2, cells_x, cells_y), F32),
            pltpu.VMEM((2, 4, ROWS, cells_y), F32),
        ]

    info = (ROWS, -(-max(parts, links) // LANES) * LANES)
    results = pl.pallas_call(
        functools.partial(kernel, parts_x, parts_y),
        out_shape=(jax.ShapeDtypeStruct(fields.shape, F32),) * 2,
        in_specs=[vmem] * 3 + [pl.BlockSpec(memory_space=pltpu.SMEM)] + [vmem] * 3
        + [pl.BlockSpec(memory_space=pl.ANY)],
        out_specs=(vmem, vmem),
        scratch_shapes=[
            pltpu.VMEM((comps, *ext), F32),
            pltpu.VMEM((comps, *ext), F32),
            pltpu.VMEM((comps, *ext), F32),
            pltpu.VMEM((comps, *ext), F32),
            pltpu.VMEM((4, *ext), F32),
            *halo_buffers(2 * comps + 1),
            *halo_buffers(comps),
            pltpu.VMEM((comps, links + ROWS, width), F32),
            pltpu.VMEM((parts, comps, ROWS, width), F32),
            pltpu.VMEM((2, parts, comps, ROWS, width), F32),
            pltpu.VMEM((parts, ROWS, width), F32),
            pltpu.VMEM((parts, ROWS, width), F32),
            pltpu.VMEM(info, jnp.int32),
            pltpu.SMEM(info, jnp.int32),
            pltpu.VMEM(rest[6].shape, BF16),
            pltpu.VMEM((chunks, 2 * cells_y, ROWS * width), BF16),
            pltpu.VMEM((links, width), jnp.int32),
            pltpu.VMEM((parts, ROWS * width, cells_y), BF16),
            pltpu.VMEM((parts, cells_x, ROWS * width), BF16),
            dma((8,)),
            dma((2, 8)),
            dma((8,)),
            dma((2, 8)),
            dma((parts,)),
            dma((2, parts)),
            dma((parts,)),
            dma((parts,)),
            dma,
            dma,
        ],
        compiler_params=pltpu.CompilerParams(
            collective_id=0, has_side_effects=True, vmem_limit_bytes=58 * 1024 * 1024
        ),
    )(fields, *rest)
    return pl.pallas_call(
        hand_over, out_shape=(jax.ShapeDtypeStruct(fields.shape, F32),) * 2, in_specs=[vmem] * 2, out_specs=(vmem, vmem)
    )(*results)


def solution(mesh):
    placed = (
        P("grp", None, "gx", "gy"),
        P("grp", "gx", "gy"),
        P("grp", None, "gx", "gy"),
        P(),
        P("grp", ("gx", "gy"), None),
        P("grp", ("gx", "gy"), None),
        P("grp", ("gx", "gy"), None),
        P("grp", ("gx", "gy"), None, None),
    )
    return jax.shard_map(
        functools.partial(body, mesh.shape["gx"], mesh.shape["gy"]),
        mesh=mesh,
        in_specs=placed,
        out_specs=(P("grp", None, "gx", "gy"), P("grp", None, "gx", "gy")),
        check_vma=False,
    )
```

```python
import functools

import jax
import jax.numpy as jnp
from jax import lax
from jax.experimental import pallas as pl
from jax.experimental.pallas import tpu as pltpu
from jax.sharding import PartitionSpec as P

ITERS = 4
SUB = 4
DT_STEP = 1.0
RELAX = 0.6
ROWS = 8
GROUP = 4
PICK = 4
LANES = 128
F32 = jnp.float32
BF16 = jnp.bfloat16


def iota(shape, dim):
    return lax.broadcasted_iota(jnp.int32, shape, dim)


def shift(value, amount, axis):
    return pltpu.roll(value, amount % value.shape[axis], axis)


def one_hot(mask):
    return jnp.where(mask, 1.0, 0.0).astype(BF16)


def step(value, amount, axis):
    tile = (ROWS, LANES)[axis]
    count = value.shape[axis] // tile
    tiles = [lax.slice_in_dim(value, k * tile, (k + 1) * tile, axis=axis) for k in range(count)]
    turned = [shift(t, amount, axis) for t in tiles]
    edge = iota(tiles[0].shape, axis) == (0 if amount > 0 else tile - 1)
    moved = [jnp.where(edge, turned[(k - amount) % count], turned[k]) for k in range(count)]
    return jnp.concatenate(moved, axis=axis)


def fold_rows(blocks):
    row = iota(blocks[0].shape, 0)
    stride = 1
    while len(blocks) > 1:
        low = row % (2 * stride) < stride
        blocks = [
            jnp.where(low, a, b) + shift(jnp.where(low, b, a), stride, 0)
            for a, b in zip(blocks[::2], blocks[1::2])
        ]
        stride *= 2
    return blocks[0]


def kernel(
    parts_x,
    parts_y,
    field_hbm,
    coef_hbm,
    force_hbm,
    element_ref,
    source_hbm,
    target_hbm,
    peer_hbm,
    map_hbm,
    field_result,
    load_result,
    field_ref,
    coef_ref,
    force_ref,
    source_ref,
    target_ref,
    peer_ref,
    field_out,
    load_out,
    input_sems,
    state,
    wave,
    load,
    base,
    stat,
    bond,
    row_send,
    col_send,
    row_recv,
    col_recv,
    corner_recv,
    load_row_send,
    load_col_send,
    load_row_recv,
    load_col_recv,
    load_corner_recv,
    spread,
    value_send,
    value_recv,
    index_send,
    index_recv,
    info,
    info_scalar,
    map_ref,
    pick_cols,
    pick_rows,
    place_cols,
    place_rows,
    halo_ss,
    halo_rs,
    load_ss,
    load_rs,
    value_ss,
    value_rs,
    index_ss,
    index_rs,
    map_sem,
    info_sem,
):
    comps, cells_x, cells_y = field_ref.shape[1:]
    links, width = source_ref.shape[1:]
    parts = parts_x * parts_y
    slots = parts * ROWS
    chunks = links // ROWS
    half_x = cells_x // 2
    span = ROWS * width
    ext_x, ext_y = state.shape[1:]
    group = lax.axis_index("grp")
    gx = lax.axis_index("gx")
    gy = lax.axis_index("gy")
    me = gx * parts_y + gy
    mesh_id = pl.DeviceIdType.MESH

    def peer_device(q):
        return {"grp": 1 - group, "gx": lax.div(q, parts_y), "gy": lax.rem(q, parts_y)}

    halves = 2 if parts_x % 2 == 0 else 1
    half = parts_x // halves

    def partner_of(k, sign):
        turn = halves - 1 - lax.div(k, half * parts_y)
        within = lax.rem(k, half * parts_y)
        along = lax.rem(lax.rem(gx, half) + sign * lax.div(within, parts_y) + half, half)
        x = lax.rem(lax.div(gx, half) + turn, halves) * half + along
        y = lax.rem(gy + sign * lax.rem(within, parts_y) + parts_y, parts_y)
        return x * parts_y + y

    def turn_of(q):
        x, y = lax.div(q, parts_y), lax.rem(q, parts_y)
        turn = halves - 1 - lax.rem(lax.div(x, half) - lax.div(gx, half) + halves, halves)
        along = lax.rem(lax.rem(x, half) - lax.rem(gx, half) + half, half)
        return (turn * half + along) * parts_y + lax.rem(y - gy + parts_y, parts_y)

    def inside(dx, dy):
        ok = None
        for pos, step, size in ((gx, dx, parts_x), (gy, dy, parts_y)):
            if step:
                test = (pos + step >= 0) & (pos + step < size)
                ok = test if ok is None else ok & test
        return ok

    steps = ((1, 0), (-1, 0), (0, -1), (0, 1), (-1, -1), (-1, 1), (1, -1), (1, 1))

    for ref in (row_recv, col_recv, corner_recv, load_row_recv, load_col_recv, load_corner_recv):
        ref[...] = jnp.zeros_like(ref)

    barrier = pltpu.get_barrier_semaphore()

    def greet(k, carry):
        q = lax.rem(me + k, parts)
        pl.semaphore_signal(barrier, inc=1, device_id=peer_device(q), device_id_type=mesh_id)
        return carry

    lax.fori_loop(0, parts, greet, 0)
    for dx, dy in steps:

        @pl.when(inside(dx, dy))
        def _(dx=dx, dy=dy):
            pl.semaphore_signal(
                barrier, inc=1, device_id={"gx": gx + dx, "gy": gy + dy}, device_id_type=mesh_id
            )

    inputs = [(peer_hbm, peer_ref), (target_hbm, target_ref), (source_hbm, source_ref)]
    inputs += [(field_hbm, field_ref), (force_hbm, force_ref), (coef_hbm, coef_ref)]
    inputs = [pltpu.make_async_copy(a, b, input_sems.at[k]) for k, (a, b) in enumerate(inputs)]
    for copy in inputs:
        copy.start()
    pltpu.make_async_copy(map_hbm, map_ref, map_sem).start()
    for ref in (spread, wave):
        ref[...] = jnp.zeros_like(ref)
    inputs[0].wait()

    def as_col(row):
        square = iota((links, links), 0) == iota((links, links), 1)
        return jnp.sum(jnp.where(square, row, 0.0), axis=1, keepdims=True)

    key_row = turn_of(peer_ref[0]).astype(F32)
    key_col = as_col(key_row)
    below, lane = iota((links, links), 0), iota((links, links), 1)
    same = (key_col == key_row) & (below < lane)
    rank_row = jnp.sum(jnp.where(same, 1.0, 0.0), axis=0, keepdims=True)
    ahead = jnp.where(same | (key_col < key_row), 1.0, 0.0)
    pos_row = jnp.sum(ahead, axis=0, keepdims=True)
    pos_col = as_col(pos_row)
    order = jnp.sum(
        jnp.where(pos_col.astype(jnp.int32) == iota((links, LANES), 1), iota((links, LANES), 0), 0),
        axis=0,
        keepdims=True,
    )
    info[0:1, :LANES] = order
    first = jnp.where(key_col.astype(jnp.int32) < iota((links, info.shape[1]), 1), 1, 0)
    info[1:2, :] = jnp.sum(first, axis=0, keepdims=True)
    info_copy = pltpu.make_async_copy(info, info_scalar, info_sem)
    info_copy.start()

    slot_row = (key_row * ROWS + rank_row).astype(jnp.int32)
    to_slot = one_hot(iota((slots, links), 0) == slot_row)
    inputs[1].wait()
    target = target_ref[0]
    target_x = (target // cells_y + 1).astype(F32).astype(BF16)
    target_y = (target % cells_y).astype(F32).astype(BF16)
    index = cells_y * (jnp.dot(to_slot, target_x, preferred_element_type=F32) - 1.0)
    index = index + jnp.dot(to_slot, target_y, preferred_element_type=F32)
    index_send[...] = index.reshape(parts, ROWS, width)

    to_place = one_hot(iota((links, links), 0) == pos_row.astype(jnp.int32))
    inputs[2].wait()
    source = source_ref[0]
    source_y = (source // (half_x * cells_y)) * cells_y + source % cells_y
    source_x = (source // cells_y) % half_x
    sorted_y = jnp.dot(to_place, source_y.astype(F32).astype(BF16), preferred_element_type=F32)
    sorted_x = jnp.dot(to_place, source_x.astype(F32).astype(BF16), preferred_element_type=F32)
    sorted_y = sorted_y.astype(jnp.int32)
    pick_rows[...] = sorted_x.astype(jnp.int32)
    def index_copy(k, q):
        return pltpu.make_async_remote_copy(
            src_ref=index_send.at[k],
            dst_ref=index_recv.at[k],
            send_sem=index_ss.at[k],
            recv_sem=index_rs.at[k],
            device_id=peer_device(q),
            device_id_type=mesh_id,
        )

    def value_copy(k, q, par):
        return pltpu.make_async_remote_copy(
            src_ref=value_send.at[k],
            dst_ref=value_recv.at[par, k],
            send_sem=value_ss.at[k],
            recv_sem=value_rs.at[par, k],
            device_id=peer_device(q),
            device_id_type=mesh_id,
        )

    field_halo = (row_send, col_send, row_recv, col_recv, corner_recv, halo_ss, halo_rs)
    load_halo = (load_row_send, load_col_send, load_row_recv, load_col_recv, load_corner_recv, load_ss, load_rs)

    def halo_copy(halo, d, par, count):
        rows, cols, rows_in, cols_in, corners_in, send, recv = halo
        dx, dy = steps[d]
        if d < 2:
            source, place = rows.at[1 - d, pl.ds(0, count)], rows_in.at[par, d, pl.ds(0, count)]
        elif d < 4:
            source, place = cols, cols_in.at[par, d - 2]
        else:
            edge = pl.ds(0, ROWS) if d < 6 else pl.ds(cells_x - ROWS, ROWS)
            source, place = cols.at[edge], corners_in.at[par, d - 4]
        return pltpu.make_async_remote_copy(
            src_ref=source,
            dst_ref=place,
            send_sem=send.at[d],
            recv_sem=recv.at[par, d],
            device_id={"gx": gx + dx, "gy": gy + dy},
            device_id_type=mesh_id,
        )

    def halo_start(halo, par, centres):
        rows, cols = halo[:2]
        lane = iota((cells_x, cells_y), 1)
        packed = jnp.zeros((cells_x, cells_y), F32)
        for q, centre in enumerate(centres):
            rows[0, q] = centre[:ROWS]
            rows[1, q] = centre[cells_x - ROWS :]
            low = (lane >= 8 * q) & (lane < 8 * q + 4)
            high = (lane >= 8 * q + 4) & (lane < 8 * q + 8)
            packed = jnp.where(low, shift(centre, 8 * q, 1), packed)
            packed = jnp.where(high, shift(centre, 8 * q + 8, 1), packed)
        cols[...] = packed
        for d, (dx, dy) in reversed(list(enumerate(steps))):

            @pl.when(inside(dx, dy))
            def _(d=d):
                halo_copy(halo, d, par, len(centres)).start()

    def halo_finish(halo, par, centres):
        rows_in, cols_in, corners_in = halo[2:5]
        for d, (dx, dy) in enumerate(steps):

            @pl.when(inside(-dx, -dy))
            def _(d=d):
                halo_copy(halo, d, par, len(centres)).wait_recv()

        upper = iota((ROWS, cells_y), 0) < SUB
        ends = [
            jnp.where(upper, corners_in[par, 0], corners_in[par, 2]),
            jnp.where(upper, corners_in[par, 1], corners_in[par, 3]),
        ]
        east = jnp.concatenate([cols_in[par, 0], ends[0]], axis=0)
        west = jnp.concatenate([cols_in[par, 1], ends[1]], axis=0)
        lane = iota((ext_x, cells_y), 1)
        wide = []
        for q, centre in enumerate(centres):
            end = jnp.where(upper, rows_in[par, 1, q], rows_in[par, 0, q])
            side = jnp.where(lane >= cells_y - SUB, shift(west, -8 * q - 8, 1), 0.0)
            side = jnp.where(lane < SUB, shift(east, -8 * q, 1), side)
            middle = jnp.concatenate([centre, end], axis=0)
            wide.append(jnp.where(keep, jnp.concatenate([middle, side], axis=1), 0.0))
        return wide

    def halo_sent(halo, count):
        for d, (dx, dy) in enumerate(steps):

            @pl.when(inside(dx, dy))
            def _(d=d):
                halo_copy(halo, d, 0, count).wait_send()

    beside_x = jnp.where(gx > 0, 1, 0) + jnp.where(gx < parts_x - 1, 1, 0)
    beside_y = jnp.where(gy > 0, 1, 0) + jnp.where(gy < parts_y - 1, 1, 0)
    pl.semaphore_wait(barrier, parts + (beside_x + 1) * (beside_y + 1) - 1)

    ext_row = iota((ext_x, ext_y), 0)
    ext_col = iota((ext_x, ext_y), 1)
    row_at = jnp.where(ext_row < cells_x + SUB, ext_row, ext_row - ext_x) + gx * cells_x
    near = (ext_col < cells_y + SUB) | (ext_col >= ext_y - SUB)
    col_at = jnp.where(ext_col < cells_y + SUB, ext_col, ext_col - ext_y) + gy * cells_y
    keep = near & (row_at >= 0) & (row_at < cells_x * parts_x)
    keep = keep & (col_at >= 0) & (col_at < cells_y * parts_y)

    nodes = ((0, 0), (1, 0), (0, 1), (1, 1))
    offsets = [(dx, dy) for dx in (0, 1, -1) for dy in (0, 1, -1)]

    for copy in inputs[3:]:
        copy.wait()
    start_values = [field_ref[0, c] for c in range(comps)]
    start_values += [force_ref[0, c] for c in range(comps)]
    start_values.append(coef_ref[0])
    halo_start(field_halo, 1, start_values)

    def send_index(k, carry):
        index_copy(k, partner_of(k, 1)).start()
        return carry

    lax.fori_loop(0, parts, send_index, 0)
    for i in range(links):
        hot = iota((2 * cells_y, width), 0) == sorted_y[i : i + 1]
        pick_cols[i // ROWS, :, i % ROWS * width : (i % ROWS + 1) * width] = one_hot(hot)
    info_copy.wait()
    wide = halo_finish(field_halo, 1, start_values)
    for c in range(comps):
        state[c] = wide[c]
        base[c] = wide[comps + c]
    coef = wide[2 * comps]
    halo_sent(field_halo, 2 * comps + 1)

    @pl.when(group == 0)
    def _():
        for k, (amount, axis) in enumerate(((-1, 0), (1, 0), (-1, 1), (1, 1))):
            stat[k] = 0.5 * (coef + shift(coef, amount, axis))

    @pl.when(group == 1)
    def _():
        stat[0] = coef
        north = shift(coef, 1, 0)
        west_coef = shift(coef, 1, 1)
        corner = shift(north, 1, 1)
        for c in range(comps):
            total = 0.0
            for node, near_coef in enumerate((coef, north, west_coef, corner)):
                k = node * comps + c
                total = total + element_ref[k, k] * near_coef
            stat[1 + c] = jnp.where(keep, RELAX / jnp.where(keep, total, 1.0), 0.0)
            base[c] = base[c] * stat[1 + c]
        near_coefs = (coef, north, west_coef, corner)
        scaled = [[-near_coef * stat[1 + c] for c in range(comps)] for near_coef in near_coefs]
        for d, offset in enumerate(offsets):
            pairs = [
                (p, q)
                for p in range(4)
                for q in range(4)
                if (nodes[q][0] - nodes[p][0], nodes[q][1] - nodes[p][1]) == offset
            ]
            for b in range(comps):
                for c in range(comps):
                    total = jnp.where(keep, 1.0, 0.0) if offset == (0, 0) and b == c else 0.0
                    for p, q in pairs:
                        total = total + element_ref[p * comps + c, q * comps + b] * scaled[p][c]
                    bond[(d * comps + b) * comps + c] = total

    def flow_sweeps(field, rhs, count):
        def sweep(i, carry):
            for c in range(comps):
                v = field[c]
                flux = rhs[c]
                for k, (amount, axis) in enumerate(((-1, 0), (1, 0), (-1, 1), (1, 1))):
                    flux = flux + stat[k] * (step(v, amount, axis) - v)
                field[c] = jnp.where(keep, v + DT_STEP * flux, 0.0)
            return carry

        lax.fori_loop(0, count, sweep, 0, unroll=True)

    def shell_sweeps(field, rhs, count):
        def sweep(rows, cols):
            totals = [rhs[c, :rows, :cols] for c in range(comps)]
            for b in range(comps):
                u = field[b]
                for dx in (0, 1, -1):
                    row = step(u, -dx, 0) if dx else u
                    for dy in (0, 1, -1):
                        near_u = step(row, -dy, 1) if dy else row
                        d = offsets.index((dx, dy))
                        for c in range(comps):
                            at = (d * comps + b) * comps + c
                            totals[c] = totals[c] + bond[at, :rows, :cols] * near_u[:rows, :cols]
            for c in range(comps):
                field[c, :rows, :cols] = totals[c]

        for _ in range(count - 1):
            sweep(ext_x, ext_y)
        sweep(cells_x, cells_y)

    def sweep_state():
        @pl.when(group == 0)
        def _():
            flow_sweeps(state, base, SUB)

        @pl.when(group == 1)
        def _():
            shell_sweeps(state, base, SUB)

    sweep_state()
    pltpu.make_async_copy(map_hbm, map_ref, map_sem).wait()

    field_copy = pltpu.make_async_copy(field_out, field_result, input_sems.at[0])

    def coupling(t, carry):
        par = lax.rem(t, 2)
        centres = [state[c, :cells_x, :cells_y] + wave[c, :cells_x, :cells_y] for c in range(comps)]
        for c in range(comps):
            field_out[0, c] = centres[c]

        @pl.when(t == ITERS - 1)
        def _():
            field_copy.start()

        @pl.when(t < ITERS - 1)
        def _():
            halo_start(field_halo, par, [field_out[0, c] for c in range(comps)])

        table = jnp.concatenate(
            [jnp.concatenate([centre[:half_x], centre[half_x:]], axis=1) for centre in centres], axis=0
        ).astype(BF16)

        def gather(i):
            at = i * ROWS
            values = jnp.dot(table, pick_cols[i], preferred_element_type=F32)
            reads = []
            for k in range(ROWS):
                lanes = slice(k * width, (k + 1) * width)
                in_row = iota((half_x, width), 0) == pick_rows[at + k : at + k + 1]
                read = []
                for c in range(comps):
                    chosen = jnp.where(in_row, values[c * half_x : (c + 1) * half_x, lanes], 0.0)
                    total = chosen[:ROWS]
                    for r in range(ROWS, half_x, ROWS):
                        total = total + chosen[r : r + ROWS]
                    read.append(total)
                reads.append(jnp.concatenate(read, axis=0).astype(BF16))
            return reads

        def interpolate(i, reads):
            at = i * ROWS
            mapped = []
            for k, read in enumerate(reads):
                block = map_ref[0, info_scalar[0, at + k]]
                mapped.append(jnp.dot(read, block, preferred_element_type=F32))
            for c in range(comps):
                spread[c, at : at + ROWS] = fold_rows([m[c * ROWS : (c + 1) * ROWS] for m in mapped])

        def send(k):
            begin = info_scalar[1, k]
            for c in range(comps):
                value_send[k, c] = spread[c, pl.ds(begin, ROWS), :]
            value_copy(k, partner_of(k, 1), par).start()

        ahead = [gather(0)]
        for i in range(chunks):
            if i + 1 < chunks:
                ahead.append(gather(i + 1))
            interpolate(i, ahead.pop(0))
            if (i + 1) % PICK == 0:
                for j in range(i + 1 - PICK, min(i + 1, parts)):
                    send(j)

        def send_rest(k, carry):
            send(k)
            return carry

        lax.fori_loop(min(chunks, parts), parts, send_rest, 0, unroll=4)

        @pl.when(t == 0)
        def _():
            def take(k, carry):
                index_copy(k, me).wait_recv()
                where = index_recv[k].astype(jnp.int32)
                in_row = where // cells_y
                where = where % cells_y
                for r in range(ROWS):
                    lanes = slice(r * width, (r + 1) * width)
                    place_rows[k, :, lanes] = one_hot(iota((cells_x, width), 0) == in_row[r : r + 1])
                    mask = jnp.where(iota((cells_y, width), 0) == where[r : r + 1], 1.0, 0.0)
                    place_cols[k, lanes] = mask.T.astype(BF16)
                return carry

            lax.fori_loop(0, parts, take, 0)

        @pl.when(t < ITERS - 1)
        def _():
            centres = [field_out[0, c] for c in range(comps)]
            wide = halo_finish(field_halo, par, centres)
            for c in range(comps):
                state[c] = wide[c]
            sweep_state()
            halo_sent(field_halo, comps)

        def weigh(k):
            weighted = []
            for r in range(ROWS):
                in_row = place_rows[k, :, r * width : (r + 1) * width]
                weighted.append(
                    jnp.concatenate(
                        [
                            jnp.broadcast_to(value_recv[par, k, c, r : r + 1], in_row.shape).astype(BF16) * in_row
                            for c in range(comps)
                        ],
                        axis=0,
                    )
                )
            return jnp.concatenate(weighted, axis=1)

        def place(i, total):
            turns = [lax.rem(i * GROUP + k + parts // 2, parts) for k in range(GROUP)]
            for k in turns:
                value_copy(k, me, par).wait_recv()
            for k in turns:
                total = total + jnp.dot(weigh(k), place_cols[k], preferred_element_type=F32)
            return total

        empty = jnp.zeros((comps * cells_x, cells_y), F32)
        applied = lax.fori_loop(0, parts // GROUP, place, empty, unroll=parts // GROUP if parts == 16 else 1)
        for c in range(comps):
            load_out[0, c] = applied[c * cells_x : (c + 1) * cells_x]

        @pl.when(t < ITERS - 1)
        def _():
            centres = [load_out[0, c] for c in range(comps)]
            halo_start(load_halo, par, centres)
            wide = halo_finish(load_halo, par, centres)
            for c in range(comps):
                load[c] = wide[c]

            @pl.when(group == 0)
            def _():
                for c in range(comps):
                    wave[c] = DT_STEP * load[c]
                flow_sweeps(wave, load, SUB - 1)

            @pl.when(group == 1)
            def _():
                for c in range(comps):
                    load[c] = load[c] * stat[1 + c]
                    wave[c] = load[c]
                shell_sweeps(wave, load, SUB - 1)

            halo_sent(load_halo, comps)

        def sent(k, carry):
            value_copy(k, me, par).wait_send()
            return carry

        lax.fori_loop(0, parts, sent, 0)
        return carry

    lax.fori_loop(0, ITERS, coupling, 0)

    load_copy = pltpu.make_async_copy(load_out, load_result, input_sems.at[1])
    load_copy.start()

    def index_sent(k, carry):
        index_copy(k, me).wait_send()
        return carry

    lax.fori_loop(0, parts, index_sent, 0)
    field_copy.wait()
    load_copy.wait()


def hand_over(field_ref, load_ref, field_out, load_out):
    field_out[...] = field_ref[...]
    load_out[...] = load_ref[...]


def body(parts_x, parts_y, fields, *rest):
    _, comps, cells_x, cells_y = fields.shape
    links, width = rest[3].shape[1:]
    parts = parts_x * parts_y
    ext = (cells_x + ROWS, cells_y + LANES)
    chunks = links // ROWS
    vmem = pl.BlockSpec(memory_space=pltpu.VMEM)
    hbm = pl.BlockSpec(memory_space=pl.ANY)
    dma = pltpu.SemaphoreType.DMA
    rest = (*rest[:5], rest[5].reshape(1, 1, links), rest[6])

    def halo_buffers(arrays):
        return [
            pltpu.VMEM((2, arrays, ROWS, cells_y), F32),
            pltpu.VMEM((cells_x, cells_y), F32),
            pltpu.VMEM((2, 2, arrays, ROWS, cells_y), F32),
            pltpu.VMEM((2, 2, cells_x, cells_y), F32),
            pltpu.VMEM((2, 4, ROWS, cells_y), F32),
        ]

    info = (ROWS, -(-max(parts, links) // LANES) * LANES)
    results = pl.pallas_call(
        functools.partial(kernel, parts_x, parts_y),
        out_shape=(jax.ShapeDtypeStruct(fields.shape, F32),) * 2,
        in_specs=[hbm] * 3 + [pl.BlockSpec(memory_space=pltpu.SMEM)] + [hbm] * 4,
        out_specs=(hbm, hbm),
        scratch_shapes=[
            pltpu.VMEM(fields.shape, F32),
            *[pltpu.VMEM(array.shape, array.dtype) for array in (rest[0], rest[1], *rest[3:6])],
            pltpu.VMEM(fields.shape, F32),
            pltpu.VMEM(fields.shape, F32),
            dma((6,)),
            pltpu.VMEM((comps, *ext), F32),
            pltpu.VMEM((comps, *ext), F32),
            pltpu.VMEM((comps, *ext), F32),
            pltpu.VMEM((comps, *ext), F32),
            pltpu.VMEM((4, *ext), F32),
            pltpu.VMEM((9 * comps * comps, *ext), F32),
            *halo_buffers(2 * comps + 1),
            *halo_buffers(comps),
            pltpu.VMEM((comps, links + ROWS, width), F32),
            pltpu.VMEM((parts, comps, ROWS, width), F32),
            pltpu.VMEM((2, parts, comps, ROWS, width), F32),
            pltpu.VMEM((parts, ROWS, width), F32),
            pltpu.VMEM((parts, ROWS, width), F32),
            pltpu.VMEM(info, jnp.int32),
            pltpu.SMEM(info, jnp.int32),
            pltpu.VMEM(rest[6].shape, BF16),
            pltpu.VMEM((chunks, 2 * cells_y, ROWS * width), BF16),
            pltpu.VMEM((links, width), jnp.int32),
            pltpu.VMEM((parts, ROWS * width, cells_y), BF16),
            pltpu.VMEM((parts, cells_x, ROWS * width), BF16),
            dma((8,)),
            dma((2, 8)),
            dma((8,)),
            dma((2, 8)),
            dma((parts,)),
            dma((2, parts)),
            dma((parts,)),
            dma((parts,)),
            dma,
            dma,
        ],
        compiler_params=pltpu.CompilerParams(
            collective_id=0, has_side_effects=True, vmem_limit_bytes=58 * 1024 * 1024
        ),
    )(fields, *rest)
    return pl.pallas_call(
        hand_over, out_shape=(jax.ShapeDtypeStruct(fields.shape, F32),) * 2, in_specs=[vmem] * 2, out_specs=(vmem, vmem)
    )(*results)


def solution(mesh):
    placed = (
        P("grp", None, "gx", "gy"),
        P("grp", "gx", "gy"),
        P("grp", None, "gx", "gy"),
        P(),
        P("grp", ("gx", "gy"), None),
        P("grp", ("gx", "gy"), None),
        P("grp", ("gx", "gy"), None),
        P("grp", ("gx", "gy"), None, None),
    )
    return jax.shard_map(
        functools.partial(body, mesh.shape["gx"], mesh.shape["gy"]),
        mesh=mesh,
        in_specs=placed,
        out_specs=(P("grp", None, "gx", "gy"), P("grp", None, "gx", "gy")),
        check_vma=False,
    )
```

```python
import functools

import jax
import jax.numpy as jnp
from jax import lax
from jax.experimental import pallas as pl
from jax.experimental.pallas import tpu as pltpu
from jax.sharding import PartitionSpec as P

ITERS = 4
SUB = 4
DT_STEP = 1.0
RELAX = 0.6
ROWS = 8
GROUP = 4
PICK = 2
LANES = 128
F32 = jnp.float32
BF16 = jnp.bfloat16


def iota(shape, dim):
    return lax.broadcasted_iota(jnp.int32, shape, dim)


def shift(value, amount, axis):
    return pltpu.roll(value, amount % value.shape[axis], axis)


def one_hot(mask):
    return jnp.where(mask, 1.0, 0.0).astype(BF16)


def step(value, amount, axis):
    tile = (ROWS, LANES)[axis]
    count = value.shape[axis] // tile
    tiles = [lax.slice_in_dim(value, k * tile, (k + 1) * tile, axis=axis) for k in range(count)]
    turned = [shift(t, amount, axis) for t in tiles]
    edge = iota(tiles[0].shape, axis) == (0 if amount > 0 else tile - 1)
    moved = [jnp.where(edge, turned[(k - amount) % count], turned[k]) for k in range(count)]
    return jnp.concatenate(moved, axis=axis)


def fold_rows(blocks):
    row = iota(blocks[0].shape, 0)
    stride = 1
    while len(blocks) > 1:
        low = row % (2 * stride) < stride
        blocks = [
            jnp.where(low, a, b) + shift(jnp.where(low, b, a), stride, 0)
            for a, b in zip(blocks[::2], blocks[1::2])
        ]
        stride *= 2
    return blocks[0]


def kernel(
    parts_x,
    parts_y,
    field_hbm,
    coef_hbm,
    force_hbm,
    element_ref,
    source_hbm,
    target_hbm,
    peer_hbm,
    map_hbm,
    field_result,
    load_result,
    field_ref,
    coef_ref,
    force_ref,
    source_ref,
    target_ref,
    peer_ref,
    field_out,
    load_out,
    input_sems,
    state,
    wave,
    load,
    base,
    stat,
    bond,
    row_send,
    col_send,
    row_recv,
    col_recv,
    corner_recv,
    load_row_send,
    load_col_send,
    load_row_recv,
    load_col_recv,
    load_corner_recv,
    spread,
    value_send,
    value_recv,
    index_send,
    index_recv,
    info,
    info_scalar,
    map_ref,
    pick_cols,
    pick_rows,
    place_cols,
    place_rows,
    halo_ss,
    halo_rs,
    load_ss,
    load_rs,
    value_ss,
    value_rs,
    index_ss,
    index_rs,
    map_sem,
    info_sem,
):
    comps, cells_x, cells_y = field_ref.shape[1:]
    links, width = source_ref.shape[1:]
    parts = parts_x * parts_y
    slots = parts * ROWS
    chunks = links // ROWS
    half_x = cells_x // 2
    span = ROWS * width
    ext_x, ext_y = state.shape[1:]
    group = lax.axis_index("grp")
    gx = lax.axis_index("gx")
    gy = lax.axis_index("gy")
    me = gx * parts_y + gy
    mesh_id = pl.DeviceIdType.MESH

    def peer_device(q):
        return {"grp": 1 - group, "gx": lax.div(q, parts_y), "gy": lax.rem(q, parts_y)}

    half = max(parts_x // 2, 1)

    def flip(place, mask, size):
        bit = 1
        result = place
        while bit < size:
            result = result + lax.rem(lax.div(mask, bit), 2) * bit * (1 - 2 * lax.rem(lax.div(place, bit), 2))
            bit *= 2
        return result

    def partner_of(k):
        back = jnp.int32(parts - 1) - k
        y = lax.rem(lax.div(back, half), parts_y)
        x = lax.div(back, half * parts_y) * half + lax.rem(back, half)
        return flip(gx, x, parts_x) * parts_y + flip(gy, y, parts_y)

    def turn_of(q):
        x = flip(lax.div(q, parts_y), gx, parts_x)
        y = flip(lax.rem(q, parts_y), gy, parts_y)
        return parts - 1 - (lax.div(x, half) * half * parts_y + y * half + lax.rem(x, half))

    def inside(dx, dy):
        ok = None
        for pos, step, size in ((gx, dx, parts_x), (gy, dy, parts_y)):
            if step:
                test = (pos + step >= 0) & (pos + step < size)
                ok = test if ok is None else ok & test
        return ok

    steps = ((1, 0), (-1, 0), (0, -1), (0, 1), (-1, -1), (-1, 1), (1, -1), (1, 1))

    for ref in (row_recv, col_recv, corner_recv, load_row_recv, load_col_recv, load_corner_recv):
        ref[...] = jnp.zeros_like(ref)

    barrier = pltpu.get_barrier_semaphore()

    def greet(k, carry):
        q = lax.rem(me + k, parts)
        pl.semaphore_signal(barrier, inc=1, device_id=peer_device(q), device_id_type=mesh_id)
        return carry

    lax.fori_loop(0, parts, greet, 0)
    for dx, dy in steps:

        @pl.when(inside(dx, dy))
        def _(dx=dx, dy=dy):
            pl.semaphore_signal(
                barrier, inc=1, device_id={"gx": gx + dx, "gy": gy + dy}, device_id_type=mesh_id
            )

    inputs = [(peer_hbm, peer_ref), (target_hbm, target_ref), (source_hbm, source_ref)]
    inputs += [(field_hbm, field_ref), (force_hbm, force_ref), (coef_hbm, coef_ref)]
    inputs = [pltpu.make_async_copy(a, b, input_sems.at[k]) for k, (a, b) in enumerate(inputs)]
    for copy in inputs:
        copy.start()
    pltpu.make_async_copy(map_hbm, map_ref, map_sem).start()
    for ref in (spread, wave):
        ref[...] = jnp.zeros_like(ref)
    inputs[0].wait()

    def as_col(row):
        square = iota((links, links), 0) == iota((links, links), 1)
        return jnp.sum(jnp.where(square, row, 0.0), axis=1, keepdims=True)

    key_row = turn_of(peer_ref[0]).astype(F32)
    key_col = as_col(key_row)
    below, lane = iota((links, links), 0), iota((links, links), 1)
    same = (key_col == key_row) & (below < lane)
    rank_row = jnp.sum(jnp.where(same, 1.0, 0.0), axis=0, keepdims=True)
    ahead = jnp.where(same | (key_col < key_row), 1.0, 0.0)
    pos_row = jnp.sum(ahead, axis=0, keepdims=True)
    pos_col = as_col(pos_row)
    order = jnp.sum(
        jnp.where(pos_col.astype(jnp.int32) == iota((links, LANES), 1), iota((links, LANES), 0), 0),
        axis=0,
        keepdims=True,
    )
    info[0:1, :LANES] = order
    first = jnp.where(key_col.astype(jnp.int32) < iota((links, info.shape[1]), 1), 1, 0)
    info[1:2, :] = jnp.sum(first, axis=0, keepdims=True)
    info_copy = pltpu.make_async_copy(info, info_scalar, info_sem)
    info_copy.start()

    slot_row = (key_row * ROWS + rank_row).astype(jnp.int32)
    to_slot = one_hot(iota((slots, links), 0) == slot_row)
    inputs[1].wait()
    target = target_ref[0]
    target_x = (target // cells_y + 1).astype(F32).astype(BF16)
    target_y = (target % cells_y).astype(F32).astype(BF16)
    index = cells_y * (jnp.dot(to_slot, target_x, preferred_element_type=F32) - 1.0)
    index = index + jnp.dot(to_slot, target_y, preferred_element_type=F32)
    index_send[...] = index.reshape(parts, ROWS, width)

    to_place = one_hot(iota((links, links), 0) == pos_row.astype(jnp.int32))
    inputs[2].wait()
    source = source_ref[0]
    source_y = (source // (half_x * cells_y)) * cells_y + source % cells_y
    source_x = (source // cells_y) % half_x
    sorted_y = jnp.dot(to_place, source_y.astype(F32).astype(BF16), preferred_element_type=F32)
    sorted_x = jnp.dot(to_place, source_x.astype(F32).astype(BF16), preferred_element_type=F32)
    sorted_y = sorted_y.astype(jnp.int32)
    pick_rows[...] = sorted_x.astype(jnp.int32)
    def index_copy(k, q):
        return pltpu.make_async_remote_copy(
            src_ref=index_send.at[k],
            dst_ref=index_recv.at[k],
            send_sem=index_ss.at[k],
            recv_sem=index_rs.at[k],
            device_id=peer_device(q),
            device_id_type=mesh_id,
        )

    def value_copy(k, q, par):
        return pltpu.make_async_remote_copy(
            src_ref=value_send.at[k],
            dst_ref=value_recv.at[par, k],
            send_sem=value_ss.at[k],
            recv_sem=value_rs.at[par, k],
            device_id=peer_device(q),
            device_id_type=mesh_id,
        )

    field_halo = (row_send, col_send, row_recv, col_recv, corner_recv, halo_ss, halo_rs)
    load_halo = (load_row_send, load_col_send, load_row_recv, load_col_recv, load_corner_recv, load_ss, load_rs)

    def side_of(count):
        lanes = 8
        while lanes < 8 * count:
            lanes *= 2
        return lanes, cells_y // lanes, cells_x * lanes // cells_y

    def halo_copy(halo, d, par, count):
        rows, cols, rows_in, cols_in, corners_in, send, recv = halo
        dx, dy = steps[d]
        side = pl.ds(0, side_of(count)[2])
        if d < 2:
            source, place = rows.at[1 - d, pl.ds(0, count)], rows_in.at[par, d, pl.ds(0, count)]
        elif d < 4:
            source, place = cols.at[side], cols_in.at[par, d - 2, side]
        else:
            source, place = cols.at[side], corners_in.at[par, d - 4, side]
        return pltpu.make_async_remote_copy(
            src_ref=source,
            dst_ref=place,
            send_sem=send.at[d],
            recv_sem=recv.at[par, d],
            device_id={"gx": gx + dx, "gy": gy + dy},
            device_id_type=mesh_id,
        )

    def halo_start(halo, par, centres):
        rows, cols = halo[:2]
        lanes, folds, height = side_of(len(centres))
        lane = iota((cells_x, cells_y), 1)
        packed = jnp.zeros((cells_x, cells_y), F32)
        for q, centre in enumerate(centres):
            rows[0, q] = centre[:ROWS]
            rows[1, q] = centre[cells_x - ROWS :]
            low = (lane >= 8 * q) & (lane < 8 * q + 4)
            high = (lane >= 8 * q + 4) & (lane < 8 * q + 8)
            packed = jnp.where(low, shift(centre, 8 * q, 1), packed)
            packed = jnp.where(high, shift(centre, 8 * q + 8, 1), packed)
        lane = iota((height, cells_y), 1)
        folded = packed[:height]
        for g in range(1, folds):
            piece = shift(packed[g * height : (g + 1) * height], g * lanes, 1)
            folded = jnp.where((lane >= g * lanes) & (lane < (g + 1) * lanes), piece, folded)
        cols[:height] = folded
        for d, (dx, dy) in reversed(list(enumerate(steps))):

            @pl.when(inside(dx, dy))
            def _(d=d):
                halo_copy(halo, d, par, len(centres)).start()

    def halo_finish(halo, par, centres):
        rows_in, cols_in, corners_in = halo[2:5]
        lanes, folds, height = side_of(len(centres))
        for d, (dx, dy) in enumerate(steps):

            @pl.when(inside(-dx, -dy))
            def _(d=d):
                halo_copy(halo, d, par, len(centres)).wait_recv()

        def unfold(folded):
            return [folded if g == 0 else shift(folded, -g * lanes, 1) for g in range(folds)]

        upper = iota((ROWS, cells_y), 0) < SUB

        def end_of(k):
            last = shift(corners_in[par, k + 2, height - ROWS : height], -(folds - 1) * lanes, 1)
            return jnp.where(upper, corners_in[par, k, :ROWS], last)

        east = jnp.concatenate([*unfold(cols_in[par, 0, :height]), end_of(0)], axis=0)
        west = jnp.concatenate([*unfold(cols_in[par, 1, :height]), end_of(1)], axis=0)
        lane = iota((ext_x, cells_y), 1)
        wide = []
        for q, centre in enumerate(centres):
            end = jnp.where(upper, rows_in[par, 1, q], rows_in[par, 0, q])
            side = jnp.where(lane >= cells_y - SUB, shift(west, -8 * q - 8, 1), 0.0)
            side = jnp.where(lane < SUB, shift(east, -8 * q, 1), side)
            middle = jnp.concatenate([centre, end], axis=0)
            wide.append(jnp.where(keep, jnp.concatenate([middle, side], axis=1), 0.0))
        return wide

    def halo_sent(halo, count):
        for d, (dx, dy) in enumerate(steps):

            @pl.when(inside(dx, dy))
            def _(d=d):
                halo_copy(halo, d, 0, count).wait_send()

    beside_x = jnp.where(gx > 0, 1, 0) + jnp.where(gx < parts_x - 1, 1, 0)
    beside_y = jnp.where(gy > 0, 1, 0) + jnp.where(gy < parts_y - 1, 1, 0)
    pl.semaphore_wait(barrier, parts + (beside_x + 1) * (beside_y + 1) - 1)

    ext_row = iota((ext_x, ext_y), 0)
    ext_col = iota((ext_x, ext_y), 1)
    row_at = jnp.where(ext_row < cells_x + SUB, ext_row, ext_row - ext_x) + gx * cells_x
    near = (ext_col < cells_y + SUB) | (ext_col >= ext_y - SUB)
    col_at = jnp.where(ext_col < cells_y + SUB, ext_col, ext_col - ext_y) + gy * cells_y
    keep = near & (row_at >= 0) & (row_at < cells_x * parts_x)
    keep = keep & (col_at >= 0) & (col_at < cells_y * parts_y)

    nodes = ((0, 0), (1, 0), (0, 1), (1, 1))
    offsets = [(dx, dy) for dx in (0, 1, -1) for dy in (0, 1, -1)]

    for copy in inputs[3:]:
        copy.wait()
    start_values = [field_ref[0, c] for c in range(comps)]
    start_values += [force_ref[0, c] for c in range(comps)]
    start_values.append(coef_ref[0])
    halo_start(field_halo, 1, start_values)

    def send_index(k, carry):
        index_copy(k, partner_of(k)).start()
        return carry

    lax.fori_loop(0, parts, send_index, 0)
    for i in range(links):
        hot = iota((2 * cells_y, width), 0) == sorted_y[i : i + 1]
        pick_cols[i // ROWS, :, i % ROWS * width : (i % ROWS + 1) * width] = one_hot(hot)
    info_copy.wait()
    wide = halo_finish(field_halo, 1, start_values)
    for c in range(comps):
        state[c] = wide[c]
        base[c] = wide[comps + c]
    coef = wide[2 * comps]
    halo_sent(field_halo, 2 * comps + 1)

    @pl.when(group == 0)
    def _():
        for k, (amount, axis) in enumerate(((-1, 0), (1, 0), (-1, 1), (1, 1))):
            stat[k] = 0.5 * (coef + shift(coef, amount, axis))

    @pl.when(group == 1)
    def _():
        stat[0] = coef
        north = shift(coef, 1, 0)
        west_coef = shift(coef, 1, 1)
        corner = shift(north, 1, 1)
        for c in range(comps):
            total = 0.0
            for node, near_coef in enumerate((coef, north, west_coef, corner)):
                k = node * comps + c
                total = total + element_ref[k, k] * near_coef
            stat[1 + c] = jnp.where(keep, RELAX / jnp.where(keep, total, 1.0), 0.0)
            base[c] = base[c] * stat[1 + c]
        near_coefs = (coef, north, west_coef, corner)
        scaled = [[-near_coef * stat[1 + c] for c in range(comps)] for near_coef in near_coefs]
        for d, offset in enumerate(offsets):
            pairs = [
                (p, q)
                for p in range(4)
                for q in range(4)
                if (nodes[q][0] - nodes[p][0], nodes[q][1] - nodes[p][1]) == offset
            ]
            for b in range(comps):
                for c in range(comps):
                    total = jnp.where(keep, 1.0, 0.0) if offset == (0, 0) and b == c else 0.0
                    for p, q in pairs:
                        total = total + element_ref[p * comps + c, q * comps + b] * scaled[p][c]
                    bond[(d * comps + b) * comps + c] = total

    def flow_sweeps(field, rhs, count):
        def sweep(i, carry):
            for c in range(comps):
                v = field[c]
                flux = rhs[c]
                for k, (amount, axis) in enumerate(((-1, 0), (1, 0), (-1, 1), (1, 1))):
                    flux = flux + stat[k] * (step(v, amount, axis) - v)
                field[c] = jnp.where(keep, v + DT_STEP * flux, 0.0)
            return carry

        lax.fori_loop(0, count, sweep, 0, unroll=True)

    def shell_sweeps(field, rhs, count):
        def sweep(rows, cols):
            totals = [rhs[c, :rows, :cols] for c in range(comps)]
            for b in range(comps):
                u = field[b]
                for dx in (0, 1, -1):
                    row = step(u, -dx, 0) if dx else u
                    for dy in (0, 1, -1):
                        near_u = step(row, -dy, 1) if dy else row
                        d = offsets.index((dx, dy))
                        for c in range(comps):
                            at = (d * comps + b) * comps + c
                            totals[c] = totals[c] + bond[at, :rows, :cols] * near_u[:rows, :cols]
            for c in range(comps):
                field[c, :rows, :cols] = totals[c]

        for _ in range(count - 1):
            sweep(ext_x, ext_y)
        sweep(cells_x, cells_y)

    def sweep_state():
        @pl.when(group == 0)
        def _():
            flow_sweeps(state, base, SUB)

        @pl.when(group == 1)
        def _():
            shell_sweeps(state, base, SUB)

    sweep_state()
    pltpu.make_async_copy(map_hbm, map_ref, map_sem).wait()

    field_copy = pltpu.make_async_copy(field_out, field_result, input_sems.at[0])

    def coupling(t, carry):
        par = lax.rem(t, 2)
        centres = [state[c, :cells_x, :cells_y] + wave[c, :cells_x, :cells_y] for c in range(comps)]
        for c in range(comps):
            field_out[0, c] = centres[c]

        @pl.when(t == ITERS - 1)
        def _():
            field_copy.start()

        table = jnp.concatenate(
            [jnp.concatenate([centre[:half_x], centre[half_x:]], axis=1) for centre in centres], axis=0
        ).astype(BF16)

        def gather(i):
            at = i * ROWS
            values = jnp.dot(table, pick_cols[i], preferred_element_type=F32)
            reads = []
            for k in range(ROWS):
                lanes = slice(k * width, (k + 1) * width)
                in_row = iota((half_x, width), 0) == pick_rows[at + k : at + k + 1]
                read = []
                for c in range(comps):
                    chosen = jnp.where(in_row, values[c * half_x : (c + 1) * half_x, lanes], 0.0)
                    total = chosen[:ROWS]
                    for r in range(ROWS, half_x, ROWS):
                        total = total + chosen[r : r + ROWS]
                    read.append(total)
                reads.append(jnp.concatenate(read, axis=0).astype(BF16))
            return reads

        def interpolate(i, reads):
            at = i * ROWS
            mapped = []
            for k, read in enumerate(reads):
                block = map_ref[0, info_scalar[0, at + k]]
                mapped.append(jnp.dot(read, block, preferred_element_type=F32))
            for c in range(comps):
                spread[c, at : at + ROWS] = fold_rows([m[c * ROWS : (c + 1) * ROWS] for m in mapped])

        def send(k):
            begin = info_scalar[1, k]
            for c in range(comps):
                value_send[k, c] = spread[c, pl.ds(begin, ROWS), :]
            value_copy(k, partner_of(k), par).start()

        ahead = [gather(0)]
        for i in range(chunks):
            if i + 1 < chunks:
                ahead.append(gather(i + 1))
            interpolate(i, ahead.pop(0))
            if (i + 1) % PICK == 0:
                for j in range(i + 1 - PICK, min(i + 1, parts)):
                    send(j)

        def send_rest(k, carry):
            send(k)
            return carry

        lax.fori_loop(min(chunks, parts), parts, send_rest, 0, unroll=8)

        @pl.when(t < ITERS - 1)
        def _():
            halo_start(field_halo, par, [field_out[0, c] for c in range(comps)])

        @pl.when(t > 0)
        def _():
            halo_sent(load_halo, comps)

        @pl.when(t == 0)
        def _():
            def take(k, carry):
                index_copy(k, me).wait_recv()
                where = index_recv[k].astype(jnp.int32)
                in_row = where // cells_y
                where = where % cells_y
                for r in range(ROWS):
                    lanes = slice(r * width, (r + 1) * width)
                    place_rows[k, :, lanes] = one_hot(iota((cells_x, width), 0) == in_row[r : r + 1])
                    mask = jnp.where(iota((cells_y, width), 0) == where[r : r + 1], 1.0, 0.0)
                    place_cols[k, lanes] = mask.T.astype(BF16)
                return carry

            lax.fori_loop(0, parts, take, 0)

        def weigh(k):
            weighted = []
            for r in range(ROWS):
                in_row = place_rows[k, :, r * width : (r + 1) * width]
                weighted.append(
                    jnp.concatenate(
                        [
                            jnp.broadcast_to(value_recv[par, k, c, r : r + 1], in_row.shape).astype(BF16) * in_row
                            for c in range(comps)
                        ],
                        axis=0,
                    )
                )
            return jnp.concatenate(weighted, axis=1)

        def place(i, total):
            turns = [lax.rem(i * GROUP + k + parts // 2, parts) for k in range(GROUP)]
            for k in turns:
                value_copy(k, me, par).wait_recv()
            for k in turns:
                total = total + jnp.dot(weigh(k), place_cols[k], preferred_element_type=F32)
            return total

        empty = jnp.zeros((comps * cells_x, cells_y), F32)
        applied = lax.fori_loop(0, parts // GROUP, place, empty, unroll=parts // GROUP if parts == 16 else 1)
        for c in range(comps):
            load_out[0, c] = applied[c * cells_x : (c + 1) * cells_x]

        def sent(k, carry):
            value_copy(k, me, par).wait_send()
            return carry

        @pl.when(t < ITERS - 1)
        def _():
            halo_start(load_halo, par, [load_out[0, c] for c in range(comps)])
            wide = halo_finish(field_halo, par, [field_out[0, c] for c in range(comps)])
            for c in range(comps):
                state[c] = wide[c]
            sweep_state()
            halo_sent(field_halo, comps)
            lax.fori_loop(0, parts, sent, 0)
            wide = halo_finish(load_halo, par, [load_out[0, c] for c in range(comps)])
            for c in range(comps):
                load[c] = wide[c]

            @pl.when(group == 0)
            def _():
                for c in range(comps):
                    wave[c] = DT_STEP * load[c]
                flow_sweeps(wave, load, SUB - 1)

            @pl.when(group == 1)
            def _():
                for c in range(comps):
                    load[c] = load[c] * stat[1 + c]
                    wave[c] = load[c]
                shell_sweeps(wave, load, SUB - 1)

        return carry

    lax.fori_loop(0, ITERS, coupling, 0)

    load_copy = pltpu.make_async_copy(load_out, load_result, input_sems.at[1])
    load_copy.start()

    def sent(k, carry):
        value_copy(k, me, 0).wait_send()
        return carry

    lax.fori_loop(0, parts, sent, 0)

    def index_sent(k, carry):
        index_copy(k, me).wait_send()
        return carry

    lax.fori_loop(0, parts, index_sent, 0)
    field_copy.wait()
    load_copy.wait()


def hand_over(field_ref, load_ref, field_out, load_out):
    field_out[...] = field_ref[...]
    load_out[...] = load_ref[...]


def body(parts_x, parts_y, fields, *rest):
    _, comps, cells_x, cells_y = fields.shape
    links, width = rest[3].shape[1:]
    parts = parts_x * parts_y
    ext = (cells_x + ROWS, cells_y + LANES)
    chunks = links // ROWS
    vmem = pl.BlockSpec(memory_space=pltpu.VMEM)
    hbm = pl.BlockSpec(memory_space=pl.ANY)
    dma = pltpu.SemaphoreType.DMA
    rest = (*rest[:5], rest[5].reshape(1, 1, links), rest[6])

    def halo_buffers(arrays):
        return [
            pltpu.VMEM((2, arrays, ROWS, cells_y), F32),
            pltpu.VMEM((cells_x, cells_y), F32),
            pltpu.VMEM((2, 2, arrays, ROWS, cells_y), F32),
            pltpu.VMEM((2, 2, cells_x, cells_y), F32),
            pltpu.VMEM((2, 4, cells_x, cells_y), F32),
        ]

    info = (ROWS, -(-max(parts, links) // LANES) * LANES)
    results = pl.pallas_call(
        functools.partial(kernel, parts_x, parts_y),
        out_shape=(jax.ShapeDtypeStruct(fields.shape, F32),) * 2,
        in_specs=[hbm] * 3 + [pl.BlockSpec(memory_space=pltpu.SMEM)] + [hbm] * 4,
        out_specs=(hbm, hbm),
        scratch_shapes=[
            pltpu.VMEM(fields.shape, F32),
            *[pltpu.VMEM(array.shape, array.dtype) for array in (rest[0], rest[1], *rest[3:6])],
            pltpu.VMEM(fields.shape, F32),
            pltpu.VMEM(fields.shape, F32),
            dma((6,)),
            pltpu.VMEM((comps, *ext), F32),
            pltpu.VMEM((comps, *ext), F32),
            pltpu.VMEM((comps, *ext), F32),
            pltpu.VMEM((comps, *ext), F32),
            pltpu.VMEM((4, *ext), F32),
            pltpu.VMEM((9 * comps * comps, *ext), F32),
            *halo_buffers(2 * comps + 1),
            *halo_buffers(comps),
            pltpu.VMEM((comps, links + ROWS, width), F32),
            pltpu.VMEM((parts, comps, ROWS, width), F32),
            pltpu.VMEM((2, parts, comps, ROWS, width), F32),
            pltpu.VMEM((parts, ROWS, width), F32),
            pltpu.VMEM((parts, ROWS, width), F32),
            pltpu.VMEM(info, jnp.int32),
            pltpu.SMEM(info, jnp.int32),
            pltpu.VMEM(rest[6].shape, BF16),
            pltpu.VMEM((chunks, 2 * cells_y, ROWS * width), BF16),
            pltpu.VMEM((links, width), jnp.int32),
            pltpu.VMEM((parts, ROWS * width, cells_y), BF16),
            pltpu.VMEM((parts, cells_x, ROWS * width), BF16),
            dma((8,)),
            dma((2, 8)),
            dma((8,)),
            dma((2, 8)),
            dma((parts,)),
            dma((2, parts)),
            dma((parts,)),
            dma((parts,)),
            dma,
            dma,
        ],
        compiler_params=pltpu.CompilerParams(
            collective_id=0, has_side_effects=True, vmem_limit_bytes=58 * 1024 * 1024
        ),
    )(fields, *rest)
    return pl.pallas_call(
        hand_over, out_shape=(jax.ShapeDtypeStruct(fields.shape, F32),) * 2, in_specs=[vmem] * 2, out_specs=(vmem, vmem)
    )(*results)


def solution(mesh):
    placed = (
        P("grp", None, "gx", "gy"),
        P("grp", "gx", "gy"),
        P("grp", None, "gx", "gy"),
        P(),
        P("grp", ("gx", "gy"), None),
        P("grp", ("gx", "gy"), None),
        P("grp", ("gx", "gy"), None),
        P("grp", ("gx", "gy"), None, None),
    )
    return jax.shard_map(
        functools.partial(body, mesh.shape["gx"], mesh.shape["gy"]),
        mesh=mesh,
        in_specs=placed,
        out_specs=(P("grp", None, "gx", "gy"), P("grp", None, "gx", "gy")),
        check_vma=False,
    )
```

```python
import functools

import jax
import jax.numpy as jnp
from jax import lax
from jax.experimental import pallas as pl
from jax.experimental.pallas import tpu as pltpu
from jax.sharding import PartitionSpec as P

ITERS = 4
SUB = 4
DT_STEP = 1.0
RELAX = 0.6
ROWS = 8
GROUP = 4
SENDS = (0, 1, 3, 5)
LANES = 128
F32 = jnp.float32
BF16 = jnp.bfloat16


def iota(shape, dim):
    return lax.broadcasted_iota(jnp.int32, shape, dim)


def shift(value, amount, axis):
    return pltpu.roll(value, amount % value.shape[axis], axis)


def one_hot(mask):
    return jnp.where(mask, 1.0, 0.0).astype(BF16)


def step(value, amount, axis):
    tile = (ROWS, LANES)[axis]
    count = value.shape[axis] // tile
    tiles = [lax.slice_in_dim(value, k * tile, (k + 1) * tile, axis=axis) for k in range(count)]
    turned = [shift(t, amount, axis) for t in tiles]
    edge = iota(tiles[0].shape, axis) == (0 if amount > 0 else tile - 1)
    moved = [jnp.where(edge, turned[(k - amount) % count], turned[k]) for k in range(count)]
    return jnp.concatenate(moved, axis=axis)


def fold_rows(blocks):
    row = iota(blocks[0].shape, 0)
    stride = 1
    while len(blocks) > 1:
        low = row % (2 * stride) < stride
        blocks = [
            jnp.where(low, a, b) + shift(jnp.where(low, b, a), stride, 0)
            for a, b in zip(blocks[::2], blocks[1::2])
        ]
        stride *= 2
    return blocks[0]


def kernel(
    parts_x,
    parts_y,
    field_hbm,
    coef_hbm,
    force_hbm,
    element_ref,
    source_hbm,
    target_hbm,
    peer_hbm,
    map_hbm,
    field_result,
    load_result,
    field_ref,
    coef_ref,
    force_ref,
    source_ref,
    target_ref,
    peer_ref,
    field_out,
    load_out,
    input_sems,
    state,
    wave,
    load,
    base,
    stat,
    bond,
    row_send,
    col_send,
    row_recv,
    col_recv,
    corner_recv,
    load_row_send,
    load_col_send,
    load_row_recv,
    load_col_recv,
    load_corner_recv,
    spread,
    value_send,
    value_recv,
    index_send,
    index_recv,
    info,
    info_scalar,
    map_ref,
    pick_cols,
    pick_rows,
    place_cols,
    place_rows,
    halo_ss,
    halo_rs,
    load_ss,
    load_rs,
    value_ss,
    value_rs,
    index_ss,
    index_rs,
    map_sem,
    info_sem,
):
    comps, cells_x, cells_y = field_ref.shape[1:]
    links, width = source_ref.shape[1:]
    parts = parts_x * parts_y
    slots = parts * ROWS
    chunks = links // ROWS
    half_x = cells_x // 2
    span = ROWS * width
    ext_x, ext_y = state.shape[1:]
    group = lax.axis_index("grp")
    gx = lax.axis_index("gx")
    gy = lax.axis_index("gy")
    me = gx * parts_y + gy
    mesh_id = pl.DeviceIdType.MESH

    def peer_device(q):
        return {"grp": 1 - group, "gx": lax.div(q, parts_y), "gy": lax.rem(q, parts_y)}

    half = max(parts_x // 2, 1)

    def flip(place, mask, size):
        bit = 1
        result = place
        while bit < size:
            result = result + lax.rem(lax.div(mask, bit), 2) * bit * (1 - 2 * lax.rem(lax.div(place, bit), 2))
            bit *= 2
        return result

    def partner_of(k):
        back = jnp.int32(parts - 1) - k
        y = lax.rem(lax.div(back, half), parts_y)
        x = lax.div(back, half * parts_y) * half + lax.rem(back, half)
        return flip(gx, x, parts_x) * parts_y + flip(gy, y, parts_y)

    def turn_of(q):
        x = flip(lax.div(q, parts_y), gx, parts_x)
        y = flip(lax.rem(q, parts_y), gy, parts_y)
        return parts - 1 - (lax.div(x, half) * half * parts_y + y * half + lax.rem(x, half))

    def inside(dx, dy):
        ok = None
        for pos, step, size in ((gx, dx, parts_x), (gy, dy, parts_y)):
            if step:
                test = (pos + step >= 0) & (pos + step < size)
                ok = test if ok is None else ok & test
        return ok

    steps = ((1, 0), (-1, 0), (0, -1), (0, 1), (-1, -1), (-1, 1), (1, -1), (1, 1))

    for ref in (row_recv, col_recv, corner_recv, load_row_recv, load_col_recv, load_corner_recv):
        ref[...] = jnp.zeros_like(ref)

    barrier = pltpu.get_barrier_semaphore()

    def greet(k, carry):
        q = partner_of(k)
        pl.semaphore_signal(barrier, inc=1, device_id=peer_device(q), device_id_type=mesh_id)
        return carry

    lax.fori_loop(0, parts, greet, 0, unroll=16)
    for dx, dy in steps:

        @pl.when(inside(dx, dy))
        def _(dx=dx, dy=dy):
            pl.semaphore_signal(
                barrier, inc=1, device_id={"gx": gx + dx, "gy": gy + dy}, device_id_type=mesh_id
            )

    inputs = [(peer_hbm, peer_ref), (target_hbm, target_ref), (source_hbm, source_ref)]
    inputs += [(field_hbm, field_ref), (force_hbm, force_ref), (coef_hbm, coef_ref)]
    inputs = [pltpu.make_async_copy(a, b, input_sems.at[k]) for k, (a, b) in enumerate(inputs)]
    for copy in inputs:
        copy.start()
    pltpu.make_async_copy(map_hbm, map_ref, map_sem).start()
    for ref in (spread, wave):
        ref[...] = jnp.zeros_like(ref)
    inputs[0].wait()

    def as_col(row):
        square = iota((links, links), 0) == iota((links, links), 1)
        return jnp.sum(jnp.where(square, row, 0.0), axis=1, keepdims=True)

    key_row = turn_of(peer_ref[0]).astype(F32)
    key_col = as_col(key_row)
    below, lane = iota((links, links), 0), iota((links, links), 1)
    same = (key_col == key_row) & (below < lane)
    rank_row = jnp.sum(jnp.where(same, 1.0, 0.0), axis=0, keepdims=True)
    ahead = jnp.where(same | (key_col < key_row), 1.0, 0.0)
    pos_row = jnp.sum(ahead, axis=0, keepdims=True)
    pos_col = as_col(pos_row)
    order = jnp.sum(
        jnp.where(pos_col.astype(jnp.int32) == iota((links, LANES), 1), iota((links, LANES), 0), 0),
        axis=0,
        keepdims=True,
    )
    info[0:1, :LANES] = order
    first = jnp.where(key_col.astype(jnp.int32) < iota((links, info.shape[1]), 1), 1, 0)
    info[1:2, :] = jnp.sum(first, axis=0, keepdims=True)
    info_copy = pltpu.make_async_copy(info, info_scalar, info_sem)
    info_copy.start()

    slot_row = (key_row * ROWS + rank_row).astype(jnp.int32)
    to_slot = one_hot(iota((slots, links), 0) == slot_row)
    inputs[1].wait()
    target = target_ref[0]
    target_x = (target // cells_y + 1).astype(F32).astype(BF16)
    target_y = (target % cells_y).astype(F32).astype(BF16)
    index = cells_y * (jnp.dot(to_slot, target_x, preferred_element_type=F32) - 1.0)
    index = index + jnp.dot(to_slot, target_y, preferred_element_type=F32)
    index_send[...] = index.reshape(parts, ROWS, width)

    to_place = one_hot(iota((links, links), 0) == pos_row.astype(jnp.int32))
    inputs[2].wait()
    source = source_ref[0]
    source_y = (source // (half_x * cells_y)) * cells_y + source % cells_y
    source_x = (source // cells_y) % half_x
    sorted_y = jnp.dot(to_place, source_y.astype(F32).astype(BF16), preferred_element_type=F32)
    sorted_x = jnp.dot(to_place, source_x.astype(F32).astype(BF16), preferred_element_type=F32)
    sorted_y = sorted_y.astype(jnp.int32)
    pick_rows[...] = sorted_x.astype(jnp.int32)
    def index_copy(k, q):
        return pltpu.make_async_remote_copy(
            src_ref=index_send.at[k],
            dst_ref=index_recv.at[k],
            send_sem=index_ss.at[k],
            recv_sem=index_rs.at[k],
            device_id=peer_device(q),
            device_id_type=mesh_id,
        )

    def value_copy(k, q, par):
        return pltpu.make_async_remote_copy(
            src_ref=value_send.at[k],
            dst_ref=value_recv.at[par, k],
            send_sem=value_ss.at[k],
            recv_sem=value_rs.at[par, k],
            device_id=peer_device(q),
            device_id_type=mesh_id,
        )

    field_halo = (row_send, col_send, row_recv, col_recv, corner_recv, halo_ss, halo_rs)
    load_halo = (load_row_send, load_col_send, load_row_recv, load_col_recv, load_corner_recv, load_ss, load_rs)

    def side_of(count):
        lanes = 8
        while lanes < 8 * count:
            lanes *= 2
        return lanes, cells_y // lanes, cells_x * lanes // cells_y

    def halo_copy(halo, d, par, count):
        rows, cols, rows_in, cols_in, corners_in, send, recv = halo
        dx, dy = steps[d]
        side = pl.ds(0, side_of(count)[2])
        if d < 2:
            source, place = rows.at[1 - d, pl.ds(0, count)], rows_in.at[par, d, pl.ds(0, count)]
        elif d < 4:
            source, place = cols.at[side], cols_in.at[par, d - 2, side]
        else:
            source, place = cols.at[side], corners_in.at[par, d - 4, side]
        return pltpu.make_async_remote_copy(
            src_ref=source,
            dst_ref=place,
            send_sem=send.at[d],
            recv_sem=recv.at[par, d],
            device_id={"gx": gx + dx, "gy": gy + dy},
            device_id_type=mesh_id,
        )

    def halo_start(halo, par, centres):
        rows, cols = halo[:2]
        lanes, folds, height = side_of(len(centres))
        lane = iota((cells_x, cells_y), 1)
        packed = jnp.zeros((cells_x, cells_y), F32)
        for q, centre in enumerate(centres):
            rows[0, q] = centre[:ROWS]
            rows[1, q] = centre[cells_x - ROWS :]
            low = (lane >= 8 * q) & (lane < 8 * q + 4)
            high = (lane >= 8 * q + 4) & (lane < 8 * q + 8)
            packed = jnp.where(low, shift(centre, 8 * q, 1), packed)
            packed = jnp.where(high, shift(centre, 8 * q + 8, 1), packed)
        lane = iota((height, cells_y), 1)
        folded = packed[:height]
        for g in range(1, folds):
            piece = shift(packed[g * height : (g + 1) * height], g * lanes, 1)
            folded = jnp.where((lane >= g * lanes) & (lane < (g + 1) * lanes), piece, folded)
        cols[:height] = folded
        for d, (dx, dy) in reversed(list(enumerate(steps))):

            @pl.when(inside(dx, dy))
            def _(d=d):
                halo_copy(halo, d, par, len(centres)).start()

    def halo_finish(halo, par, centres):
        rows_in, cols_in, corners_in = halo[2:5]
        lanes, folds, height = side_of(len(centres))
        for d, (dx, dy) in enumerate(steps):

            @pl.when(inside(-dx, -dy))
            def _(d=d):
                halo_copy(halo, d, par, len(centres)).wait_recv()

        def unfold(folded):
            return [folded if g == 0 else shift(folded, -g * lanes, 1) for g in range(folds)]

        upper = iota((ROWS, cells_y), 0) < SUB

        def end_of(k):
            last = shift(corners_in[par, k + 2, height - ROWS : height], -(folds - 1) * lanes, 1)
            return jnp.where(upper, corners_in[par, k, :ROWS], last)

        east = jnp.concatenate([*unfold(cols_in[par, 0, :height]), end_of(0)], axis=0)
        west = jnp.concatenate([*unfold(cols_in[par, 1, :height]), end_of(1)], axis=0)
        lane = iota((ext_x, cells_y), 1)
        wide = []
        for q, centre in enumerate(centres):
            end = jnp.where(upper, rows_in[par, 1, q], rows_in[par, 0, q])
            side = jnp.where(lane >= cells_y - SUB, shift(west, -8 * q - 8, 1), 0.0)
            side = jnp.where(lane < SUB, shift(east, -8 * q, 1), side)
            middle = jnp.concatenate([centre, end], axis=0)
            wide.append(jnp.where(keep, jnp.concatenate([middle, side], axis=1), 0.0))
        return wide

    def halo_sent(halo, count):
        for d, (dx, dy) in enumerate(steps):

            @pl.when(inside(dx, dy))
            def _(d=d):
                halo_copy(halo, d, 0, count).wait_send()

    beside_x = jnp.where(gx > 0, 1, 0) + jnp.where(gx < parts_x - 1, 1, 0)
    beside_y = jnp.where(gy > 0, 1, 0) + jnp.where(gy < parts_y - 1, 1, 0)
    pl.semaphore_wait(barrier, parts + (beside_x + 1) * (beside_y + 1) - 1)

    ext_row = iota((ext_x, ext_y), 0)
    ext_col = iota((ext_x, ext_y), 1)
    row_at = jnp.where(ext_row < cells_x + SUB, ext_row, ext_row - ext_x) + gx * cells_x
    near = (ext_col < cells_y + SUB) | (ext_col >= ext_y - SUB)
    col_at = jnp.where(ext_col < cells_y + SUB, ext_col, ext_col - ext_y) + gy * cells_y
    keep = near & (row_at >= 0) & (row_at < cells_x * parts_x)
    keep = keep & (col_at >= 0) & (col_at < cells_y * parts_y)

    nodes = ((0, 0), (1, 0), (0, 1), (1, 1))
    offsets = [(dx, dy) for dx in (0, 1, -1) for dy in (0, 1, -1)]

    for copy in inputs[3:]:
        copy.wait()
    start_values = [field_ref[0, c] for c in range(comps)]
    start_values += [force_ref[0, c] for c in range(comps)]
    start_values.append(coef_ref[0])
    halo_start(field_halo, 1, start_values)

    def send_index(k, carry):
        index_copy(k, partner_of(k)).start()
        return carry

    lax.fori_loop(0, parts, send_index, 0)
    for i in range(links):
        hot = iota((2 * cells_y, width), 0) == sorted_y[i : i + 1]
        pick_cols[i // ROWS, :, i % ROWS * width : (i % ROWS + 1) * width] = one_hot(hot)
    info_copy.wait()
    wide = halo_finish(field_halo, 1, start_values)
    for c in range(comps):
        state[c] = wide[c]
        base[c] = wide[comps + c]
    coef = wide[2 * comps]
    halo_sent(field_halo, 2 * comps + 1)

    @pl.when(group == 0)
    def _():
        for k, (amount, axis) in enumerate(((-1, 0), (1, 0), (-1, 1), (1, 1))):
            stat[k] = 0.5 * (coef + shift(coef, amount, axis))

    @pl.when(group == 1)
    def _():
        stat[0] = coef
        north = shift(coef, 1, 0)
        west_coef = shift(coef, 1, 1)
        corner = shift(north, 1, 1)
        for c in range(comps):
            total = 0.0
            for node, near_coef in enumerate((coef, north, west_coef, corner)):
                k = node * comps + c
                total = total + element_ref[k, k] * near_coef
            stat[1 + c] = jnp.where(keep, RELAX / jnp.where(keep, total, 1.0), 0.0)
            base[c] = base[c] * stat[1 + c]
        near_coefs = (coef, north, west_coef, corner)
        scaled = [[-near_coef * stat[1 + c] for c in range(comps)] for near_coef in near_coefs]
        for d, offset in enumerate(offsets):
            pairs = [
                (p, q)
                for p in range(4)
                for q in range(4)
                if (nodes[q][0] - nodes[p][0], nodes[q][1] - nodes[p][1]) == offset
            ]
            for b in range(comps):
                for c in range(comps):
                    total = jnp.where(keep, 1.0, 0.0) if offset == (0, 0) and b == c else 0.0
                    for p, q in pairs:
                        total = total + element_ref[p * comps + c, q * comps + b] * scaled[p][c]
                    bond[(d * comps + b) * comps + c] = total

    def flow_sweeps(field, rhs, count):
        def sweep(i, carry):
            for c in range(comps):
                v = field[c]
                flux = rhs[c]
                for k, (amount, axis) in enumerate(((-1, 0), (1, 0), (-1, 1), (1, 1))):
                    flux = flux + stat[k] * (step(v, amount, axis) - v)
                field[c] = jnp.where(keep, v + DT_STEP * flux, 0.0)
            return carry

        lax.fori_loop(0, count, sweep, 0, unroll=True)

    def shell_sweeps(field, rhs, count):
        def sweep(rows, cols):
            totals = [rhs[c, :rows, :cols] for c in range(comps)]
            for b in range(comps):
                u = field[b]
                for dx in (0, 1, -1):
                    row = step(u, -dx, 0) if dx else u
                    for dy in (0, 1, -1):
                        near_u = step(row, -dy, 1) if dy else row
                        d = offsets.index((dx, dy))
                        for c in range(comps):
                            at = (d * comps + b) * comps + c
                            totals[c] = totals[c] + bond[at, :rows, :cols] * near_u[:rows, :cols]
            for c in range(comps):
                field[c, :rows, :cols] = totals[c]

        for _ in range(count - 1):
            sweep(ext_x, ext_y)
        sweep(cells_x, cells_y)

    def sweep_state():
        @pl.when(group == 0)
        def _():
            flow_sweeps(state, base, SUB)

        @pl.when(group == 1)
        def _():
            shell_sweeps(state, base, SUB)

    sweep_state()
    pltpu.make_async_copy(map_hbm, map_ref, map_sem).wait()

    field_copy = pltpu.make_async_copy(field_out, field_result, input_sems.at[0])

    def coupling(t, carry):
        par = lax.rem(t, 2)
        centres = [state[c, :cells_x, :cells_y] + wave[c, :cells_x, :cells_y] for c in range(comps)]
        for c in range(comps):
            field_out[0, c] = centres[c]

        @pl.when(t == ITERS - 1)
        def _():
            field_copy.start()

        table = jnp.concatenate(
            [jnp.concatenate([centre[:half_x], centre[half_x:]], axis=1) for centre in centres], axis=0
        ).astype(BF16)

        def gather(i):
            at = i * ROWS
            values = jnp.dot(table, pick_cols[i], preferred_element_type=F32)
            reads = []
            for k in range(ROWS):
                lanes = slice(k * width, (k + 1) * width)
                in_row = iota((half_x, width), 0) == pick_rows[at + k : at + k + 1]
                read = []
                for c in range(comps):
                    chosen = jnp.where(in_row, values[c * half_x : (c + 1) * half_x, lanes], 0.0)
                    total = chosen[:ROWS]
                    for r in range(ROWS, half_x, ROWS):
                        total = total + chosen[r : r + ROWS]
                    read.append(total)
                reads.append(jnp.concatenate(read, axis=0).astype(BF16))
            return reads

        def interpolate(i, reads):
            at = i * ROWS
            mapped = []
            for k, read in enumerate(reads):
                block = map_ref[0, info_scalar[0, at + k]]
                mapped.append(jnp.dot(read, block, preferred_element_type=F32))
            for c in range(comps):
                spread[c, at : at + ROWS] = fold_rows([m[c * ROWS : (c + 1) * ROWS] for m in mapped])

        def send(k):
            begin = info_scalar[1, k]
            for c in range(comps):
                value_send[k, c] = spread[c, pl.ds(begin, ROWS), :]
            value_copy(k, partner_of(k), par).start()

        ahead = [gather(0)]
        ready = 0
        for i in range(chunks):
            if i + 1 < chunks:
                ahead.append(gather(i + 1))
            interpolate(i, ahead.pop(0))
            if i in SENDS or i + 1 == chunks:
                for j in range(ready, min(i + 1, parts)):
                    send(j)
                ready = i + 1

        def send_rest(k, carry):
            send(k)
            return carry

        lax.fori_loop(min(chunks, parts), parts, send_rest, 0, unroll=8)

        @pl.when(t < ITERS - 1)
        def _():
            halo_start(field_halo, par, [field_out[0, c] for c in range(comps)])

        @pl.when(t > 0)
        def _():
            halo_sent(load_halo, comps)

        @pl.when(t == 0)
        def _():
            def take(k, carry):
                index_copy(k, me).wait_recv()
                where = index_recv[k].astype(jnp.int32)
                in_row = where // cells_y
                where = where % cells_y
                for r in range(ROWS):
                    lanes = slice(r * width, (r + 1) * width)
                    place_rows[k, :, lanes] = one_hot(iota((cells_x, width), 0) == in_row[r : r + 1])
                    mask = jnp.where(iota((cells_y, width), 0) == where[r : r + 1], 1.0, 0.0)
                    place_cols[k, lanes] = mask.T.astype(BF16)
                return carry

            lax.fori_loop(0, parts, take, 0)

            def index_sent(k, carry):
                index_copy(k, me).wait_send()
                return carry

            lax.fori_loop(0, parts, index_sent, 0)

        def weigh(k):
            weighted = []
            for r in range(ROWS):
                in_row = place_rows[k, :, r * width : (r + 1) * width]
                weighted.append(
                    jnp.concatenate(
                        [
                            jnp.broadcast_to(value_recv[par, k, c, r : r + 1], in_row.shape).astype(BF16) * in_row
                            for c in range(comps)
                        ],
                        axis=0,
                    )
                )
            return jnp.concatenate(weighted, axis=1)

        def place(i, total):
            turns = [lax.rem(i * GROUP + k + parts // 2, parts) for k in range(GROUP)]
            for k in turns:
                value_copy(k, me, par).wait_recv()
            for k in turns:
                total = total + jnp.dot(weigh(k), place_cols[k], preferred_element_type=F32)
            return total

        def sent(k, carry):
            value_copy(k, me, par).wait_send()
            return carry

        empty = jnp.zeros((comps * cells_x, cells_y), F32)
        last = parts // GROUP - 1
        applied = lax.fori_loop(0, last, place, empty, unroll=max(last, 1) if parts <= 32 else 1)

        @pl.when(t == ITERS - 1)
        def _():
            lax.fori_loop(0, parts, sent, 0)

        applied = place(last, applied)
        for c in range(comps):
            load_out[0, c] = applied[c * cells_x : (c + 1) * cells_x]

        @pl.when(t < ITERS - 1)
        def _():
            halo_start(load_halo, par, [load_out[0, c] for c in range(comps)])
            wide = halo_finish(field_halo, par, [field_out[0, c] for c in range(comps)])
            for c in range(comps):
                state[c] = wide[c]
            sweep_state()
            halo_sent(field_halo, comps)
            lax.fori_loop(0, parts, sent, 0)
            wide = halo_finish(load_halo, par, [load_out[0, c] for c in range(comps)])
            for c in range(comps):
                load[c] = wide[c]

            @pl.when(group == 0)
            def _():
                for c in range(comps):
                    wave[c] = DT_STEP * load[c]
                flow_sweeps(wave, load, SUB - 1)

            @pl.when(group == 1)
            def _():
                for c in range(comps):
                    load[c] = load[c] * stat[1 + c]
                    wave[c] = load[c]
                shell_sweeps(wave, load, SUB - 1)

        return carry

    lax.fori_loop(0, ITERS, coupling, 0)

    load_copy = pltpu.make_async_copy(load_out, load_result, input_sems.at[1])
    load_copy.start()
    field_copy.wait()
    load_copy.wait()


def hand_over(field_ref, load_ref, field_out, load_out):
    field_out[...] = field_ref[...]
    load_out[...] = load_ref[...]


def body(parts_x, parts_y, fields, *rest):
    _, comps, cells_x, cells_y = fields.shape
    links, width = rest[3].shape[1:]
    parts = parts_x * parts_y
    ext = (cells_x + ROWS, cells_y + LANES)
    chunks = links // ROWS
    vmem = pl.BlockSpec(memory_space=pltpu.VMEM)
    hbm = pl.BlockSpec(memory_space=pl.ANY)
    dma = pltpu.SemaphoreType.DMA
    rest = (*rest[:5], rest[5].reshape(1, 1, links), rest[6])

    def halo_buffers(arrays):
        return [
            pltpu.VMEM((2, arrays, ROWS, cells_y), F32),
            pltpu.VMEM((cells_x, cells_y), F32),
            pltpu.VMEM((2, 2, arrays, ROWS, cells_y), F32),
            pltpu.VMEM((2, 2, cells_x, cells_y), F32),
            pltpu.VMEM((2, 4, cells_x, cells_y), F32),
        ]

    info = (ROWS, -(-max(parts, links) // LANES) * LANES)
    results = pl.pallas_call(
        functools.partial(kernel, parts_x, parts_y),
        out_shape=(jax.ShapeDtypeStruct(fields.shape, F32),) * 2,
        in_specs=[hbm] * 3 + [pl.BlockSpec(memory_space=pltpu.SMEM)] + [hbm] * 4,
        out_specs=(hbm, hbm),
        scratch_shapes=[
            pltpu.VMEM(fields.shape, F32),
            *[pltpu.VMEM(array.shape, array.dtype) for array in (rest[0], rest[1], *rest[3:6])],
            pltpu.VMEM(fields.shape, F32),
            pltpu.VMEM(fields.shape, F32),
            dma((6,)),
            pltpu.VMEM((comps, *ext), F32),
            pltpu.VMEM((comps, *ext), F32),
            pltpu.VMEM((comps, *ext), F32),
            pltpu.VMEM((comps, *ext), F32),
            pltpu.VMEM((4, *ext), F32),
            pltpu.VMEM((9 * comps * comps, *ext), F32),
            *halo_buffers(2 * comps + 1),
            *halo_buffers(comps),
            pltpu.VMEM((comps, links + ROWS, width), F32),
            pltpu.VMEM((parts, comps, ROWS, width), F32),
            pltpu.VMEM((2, parts, comps, ROWS, width), F32),
            pltpu.VMEM((parts, ROWS, width), F32),
            pltpu.VMEM((parts, ROWS, width), F32),
            pltpu.VMEM(info, jnp.int32),
            pltpu.SMEM(info, jnp.int32),
            pltpu.VMEM(rest[6].shape, BF16),
            pltpu.VMEM((chunks, 2 * cells_y, ROWS * width), BF16),
            pltpu.VMEM((links, width), jnp.int32),
            pltpu.VMEM((parts, ROWS * width, cells_y), BF16),
            pltpu.VMEM((parts, cells_x, ROWS * width), BF16),
            dma((8,)),
            dma((2, 8)),
            dma((8,)),
            dma((2, 8)),
            dma((parts,)),
            dma((2, parts)),
            dma((parts,)),
            dma((parts,)),
            dma,
            dma,
        ],
        compiler_params=pltpu.CompilerParams(
            collective_id=0, has_side_effects=True, vmem_limit_bytes=58 * 1024 * 1024
        ),
    )(fields, *rest)
    return pl.pallas_call(
        hand_over, out_shape=(jax.ShapeDtypeStruct(fields.shape, F32),) * 2, in_specs=[vmem] * 2, out_specs=(vmem, vmem)
    )(*results)


def solution(mesh):
    placed = (
        P("grp", None, "gx", "gy"),
        P("grp", "gx", "gy"),
        P("grp", None, "gx", "gy"),
        P(),
        P("grp", ("gx", "gy"), None),
        P("grp", ("gx", "gy"), None),
        P("grp", ("gx", "gy"), None),
        P("grp", ("gx", "gy"), None, None),
    )
    return jax.shard_map(
        functools.partial(body, mesh.shape["gx"], mesh.shape["gy"]),
        mesh=mesh,
        in_specs=placed,
        out_specs=(P("grp", None, "gx", "gy"), P("grp", None, "gx", "gy")),
        check_vma=False,
    )
```
